32 devices in a mesh: sub: 4 (over x, core), slab: 8 (over z, y).
Axes of the slice: x: 2, y: 2, z: 4, core: 2. Of those that a mesh axis runs over, the one named last changes fastest.
Arguments:
- source: float32 [4, 256, 256, 256], P('sub', 'slab'), may hold values from -6 to 6
- coarse: float32 [2, 4, 256, 256, 256], P(None, 'sub', 'slab'), may hold values from -4 to 4
- rho: float32 [4], replicated, may hold values from 0.3 to 45, as said below
- basis_x: float32 [256, 256], replicated, may hold values from -0.375 to 0.375
- basis_y: float32 [256, 256], replicated, may hold values from -0.375 to 0.375
- basis_z: float32 [256, 256], replicated, may hold values from -0.375 to 0.375
- eigen_x: float32 [256], replicated, may hold values from 0.1 to 3
- eigen_y: float32 [256], replicated, may hold values from 0.1 to 3
- eigen_z: float32 [256], replicated, may hold values from 0.1 to 3
- face_stiff: float32 [256, 256], replicated, may hold values from 0.2 to 2
Outputs:
- solution: float32 [4, 256, 256, 256], P('sub', 'slab')
- multipliers: float32 [4, 256, 256], P('sub', 'slab')
- jump: float32 [4, 256, 256], P('sub', 'slab')
The draws below stay inside these ranges and needn't reach their ends.
Inputs may be any that keep to these rules, and one draw needn't show every extreme that they name: `rho`: positive coefficient of each subdomain.
All inputs are finite; a program needn't handle non-finite values.
Results may differ from the reference program's by a relative error of at most 0.00014.
Values sent between devices are 32-bit elements; how exact they have to be, the bound alone decides.
A program may use at most 128 MiB of HBM per device.

```python
import math
import jax
import jax.numpy as jnp
from jax import lax

N = 256
ITERS = 2
SUBS = 4


def draw_rho(key, part):
    place = jnp.arange(SUBS, dtype=jnp.float32) / max(SUBS - 1, 1)
    jitter = jax.random.uniform(key, (SUBS,), jnp.float32, 0.7, 1.4)
    return jnp.exp(jnp.log(10.0) * place) * jitter


def steps_of(rng, shape, shards, low, top_value):
    factor_of, own = 1.0, jax.random.fold_in(rng, 6)
    for axis_at, shards_of in shards:
        draws = jnp.exp(jax.random.uniform(jax.random.fold_in(own, axis_at), (shards_of,), jnp.float32, low / len(shards), top_value / len(shards)))
        factor_of = factor_of * jnp.repeat(draws, shape[axis_at] // shards_of).reshape([-1 if axis == axis_at else 1 for axis in range(len(shape))])
    return factor_of


def scatter_about(stream_key, shape, scale, reach, split=(), kind=jnp.bfloat16):
    gain = steps_of(stream_key, shape, split, -0.22, 0.18) if split else 1.0
    result = jax.random.normal(stream_key, shape, jnp.float32) * scale * gain
    return jnp.minimum(jnp.maximum(result, -reach), reach).astype(kind)


def setup_inputs(seed: int = 0) -> dict:
    seeds = jax.random.split(jax.random.key(seed), 11)
    return {
        "source": scatter_about(seeds[0], (SUBS, N, N, N), 1.0, 6.0, ((0, 4), (1, 8)), jnp.float32),
        "coarse": scatter_about(seeds[1], (ITERS, SUBS, N, N, N), 0.5, 4.0, ((1, 4), (2, 8)), jnp.float32),
        "rho": draw_rho(jax.random.fold_in(seeds[10], 71), 0),
        "basis_x": scatter_about(seeds[3], (N, N), N ** -0.5, 0.375, (), jnp.float32),
        "basis_y": scatter_about(seeds[4], (N, N), N ** -0.5, 0.375, (), jnp.float32),
        "basis_z": scatter_about(seeds[5], (N, N), N ** -0.5, 0.375, (), jnp.float32),
        "eigen_x": jnp.clip(jnp.exp(jax.random.uniform(seeds[6], (N,), jnp.float32, math.log(0.1), math.log(3.0))), 0.1, 3.0),
        "eigen_y": jnp.clip(jnp.exp(jax.random.uniform(seeds[7], (N,), jnp.float32, math.log(0.1), math.log(3.0))), 0.1, 3.0),
        "eigen_z": jnp.clip(jnp.exp(jax.random.uniform(seeds[8], (N,), jnp.float32, math.log(0.1), math.log(3.0))), 0.1, 3.0),
        "face_stiff": jnp.clip(jnp.exp(jax.random.uniform(seeds[9], (N, N), jnp.float32, math.log(0.2), math.log(2.0))), 0.2, 2.0),
    }


HI = lax.Precision.HIGHEST


def forward(field, basis_x, basis_y, basis_z):
    part = jnp.einsum('xyz,zk->xyk', field, basis_z, precision=HI)
    part = jnp.einsum('xyk,yj->xjk', part, basis_y, precision=HI)
    return jnp.einsum('xjk,xi->ijk', part, basis_x, precision=HI)


def inverse(modes, basis_x, basis_y, basis_z):
    part = jnp.einsum('ijk,xi->xjk', modes, basis_x, precision=HI)
    part = jnp.einsum('xjk,yj->xyk', part, basis_y, precision=HI)
    return jnp.einsum('xyk,zk->xyz', part, basis_z, precision=HI)


def reference(source, coarse, rho, basis_x, basis_y, basis_z, eigen_x, eigen_y, eigen_z, face_stiff):
    denom = eigen_x[:, None, None] + eigen_y[None, :, None] + eigen_z[None, None, :]

    def solve_one(pair):
        field, coeff = pair
        modes = forward(field, basis_x, basis_y, basis_z) / (denom * coeff)
        return inverse(modes, basis_x, basis_y, basis_z)

    weights = 0.5 * (rho + jnp.roll(rho, -1))
    multipliers = jnp.zeros((SUBS, N, N), jnp.float32)
    solution = source
    jump = multipliers
    for step in range(ITERS):
        earlier = jnp.roll(multipliers, 1, axis=0)
        load = source + coarse[step]
        load = load.at[:, :, :, N - 1].add(-multipliers)
        load = load.at[:, :, :, 0].add(earlier)
        solution = lax.map(solve_one, (load, rho))
        jump = solution[:, :, :, N - 1] - jnp.roll(solution[:, :, :, 0], -1, axis=0)
        face = jnp.einsum('sxy,yj->sxj', jump, basis_y, precision=HI)
        face = jnp.einsum('sxj,xi->sij', face, basis_x, precision=HI)
        face = face * face_stiff[None]
        face = jnp.einsum('sij,xi->sxj', face, basis_x, precision=HI)
        face = jnp.einsum('sxj,yj->sxy', face, basis_y, precision=HI)
        search = weights[:, None, None] * face
        alpha = jnp.sum(jump * search) / (jnp.sum(search * search) + 1e-6)
        multipliers = multipliers + alpha * search
    return solution, multipliers, jump
```

```python
import functools

import jax
import jax.numpy as jnp
from jax import lax
from jax.experimental import pallas as pl
from jax.experimental.pallas import tpu as pltpu
from jax.sharding import PartitionSpec as P

ITERS = 2
GROUP = 4
TILE = 8
LANES = 128

HI = lax.Precision.HIGHEST
F32 = jnp.float32
BF16 = jnp.bfloat16
MESH = pl.DeviceIdType.MESH


def split(value):
    top = value.astype(BF16)
    return top, (value - top.astype(F32)).astype(BF16)


def as_left(value):
    top, low = split(value)
    return jnp.concatenate([top, top, low], axis=1)


def as_right(value):
    top, low = split(value)
    return jnp.concatenate([top, low, top], axis=0)


def dot(left, right):
    return jnp.dot(left, right, preferred_element_type=F32)


def exact(left, right):
    return jnp.dot(left, right, preferred_element_type=F32, precision=HI)


def feti_kernel(
    subs, slabs, rows, width,
    source, coarse, rho, basis_x, basis_y, basis_z, eigen_x, eigen_y, eigen_z, stiff,
    fields, own_mult, own_jump,
    source_in, coarse_in, sent, lines, spread, got,
    z_right, zt_right, yt_left, xt_left, x_left, x_t, y_t, stiff_t,
    pair_eigen, yz_eigen, x_column, z_column, first_column, last_column,
    share_first, share_last, beside, parts_in, gathered, ends_in,
    jump_t, search_t, search_in, mult_t, force, edge, sums_out, sums_in,
    in_sem, own_sem, out_sem, fwd_send, fwd_recv, inv_send, inv_recv,
    part_send, part_recv, all_send, all_recv, side_send, side_recv, sum_send, sum_recv,
):
    me = lax.axis_index("slab")
    sub = lax.axis_index("sub")
    chunks = rows // TILE
    lanes = min(width, LANES)
    halves = width // lanes
    step_rows = TILE * halves
    ahead = lambda m: lax.rem(me + m, slabs)
    behind = lambda m: lax.rem(me + slabs - m, slabs)
    next_sub = lax.rem(sub + 1, subs)
    last_sub = lax.rem(sub + subs - 1, subs)
    own_rho = rho[sub]
    weight = 0.5 * (own_rho + rho[next_sub])

    def remote(src, dst, send, recv, target):
        return pltpu.make_async_remote_copy(
            src_ref=src, dst_ref=dst, send_sem=send, recv_sem=recv, device_id=target, device_id_type=MESH
        )

    def fetch(which, g, slot):
        at = pl.ds(g * GROUP, GROUP)
        return (
            pltpu.make_async_copy(source.at[0, at], source_in.at[slot], in_sem.at[0, slot]),
            pltpu.make_async_copy(coarse.at[which, 0, at], coarse_in.at[slot], in_sem.at[1, slot]),
        )

    def start(copies):
        for copy in copies:
            copy.start()

    start(fetch(1, 0, 0))

    barrier = pltpu.get_barrier_semaphore()
    for m in range(1, slabs):
        pl.semaphore_signal(barrier, inc=1, device_id=(sub, ahead(m)), device_id_type=MESH)
    for m in range(1, subs):
        pl.semaphore_signal(barrier, inc=1, device_id=(lax.rem(sub + m, subs), me), device_id_type=MESH)

    z_right[...] = as_right(basis_z[...])
    y_t[...] = basis_y[...].T
    yt_left[...] = as_left(y_t[...])

    pl.semaphore_wait(barrier, slabs + subs - 2)

    def forward(m, c, first, count):
        at = pl.ds(first * step_rows, count * step_rows)
        d = ahead(m)
        return remote(
            sent.at[d * chunks + c, at], lines.at[c * slabs + me, at],
            fwd_send.at[c, m], fwd_recv.at[c, m], (sub, d),
        )

    def forward_all(c, first, count):
        for m in range(1, slabs):
            forward(m, c, first, count).start()

    def transform(which, store, after):
        steps = rows // GROUP

        def step(g, carry):
            slot = lax.rem(g, 2)

            @pl.when(g + 1 < steps)
            def _():
                start(fetch(which, g + 1, 1 - slot))

            for copy in fetch(which, g, slot):
                copy.wait()
            for r in range(GROUP):
                load = source_in[slot, r] + coarse_in[slot, r]
                part = dot(as_left(load), z_right[...])
                part = dot(yt_left[...], as_right(part))
                for h in range(halves):
                    at = pl.ds(pl.multiple_of((g * GROUP + r) * step_rows + h * TILE, TILE), TILE)
                    store[:, at, :] = part[:, h * lanes : (h + 1) * lanes].reshape(width // TILE, TILE, lanes)
            after(g)
            return carry

        lax.fori_loop(0, steps, step, 0)

    transform(1, sent, lambda g: forward_all(0, g * GROUP, GROUP))
    if chunks > 1:
        forward_all(1, 0, rows)

    keep = lambda c: pltpu.make_async_copy(sent.at[me * chunks + c], lines.at[c * slabs + me], own_sem.at[c])
    for c in range(chunks):
        keep(c).start()

    start(fetch(0, 0, 0))
    square = lambda row: jnp.broadcast_to(row, (width, width))
    down = lambda row: square(row).T
    y_column = down(eigen_y[...])
    pair_eigen[...] = y_column + eigen_x[...]
    yz_eigen[...] = y_column + eigen_z[...]
    x_column[...] = down(eigen_x[...])
    z_column[...] = down(eigen_z[...])
    first_column[...] = down(basis_z[0:1, :])
    last_column[...] = down(basis_z[width - 1 : width, :])
    x_t[...] = basis_x[...].T
    xt_left[...] = as_left(x_t[...])
    x_left[...] = as_left(basis_x[...])
    zt_right[...] = as_right(basis_z[...].T)
    stiff_t[...] = stiff[...].T

    transform(0, spread, lambda g: None)

    def line_of(ref, q, at):
        return jnp.concatenate(
            [ref[q, pl.ds(h * TILE + at, rows, stride=step_rows), :] for h in range(halves)], axis=1
        )

    own_x = as_right(basis_x[pl.ds(pl.multiple_of(me * rows, TILE), rows), :])

    def partial_edges(jg, carry):
        at_j = pl.ds(pl.multiple_of(jg * TILE, TILE), TILE)
        eigen = pair_eigen[at_j, :]
        firsts, lasts = [], []
        for at in range(TILE):
            left = as_right_first(line_of(spread, jg, at))
            hat = lax.dot_general(left, own_x, (((0,), (0,)), ((), ())), preferred_element_type=F32)
            modes = hat / (eigen[at : at + 1, :] + z_column[...])
            firsts.append(jnp.sum(modes * first_column[...], axis=0, keepdims=True))
            lasts.append(jnp.sum(modes * last_column[...], axis=0, keepdims=True))
        share_first[at_j, :] = jnp.concatenate(firsts, axis=0) / own_rho
        share_last[at_j, :] = jnp.concatenate(lasts, axis=0) / own_rho
        return carry

    lax.fori_loop(0, width // TILE, partial_edges, 0)

    aside = remote(share_first, beside, side_send.at[0], side_recv.at[0], (last_sub, me))
    aside.start()
    aside.wait()
    share_last[...] = share_last[...] - beside[...]

    own_at = pl.ds(pl.multiple_of(me * rows, TILE), rows)
    scatter = [
        remote(
            share_last.at[pl.ds(pl.multiple_of(ahead(m) * rows, TILE), rows)], parts_in.at[m],
            part_send.at[m], part_recv.at[m], (sub, ahead(m)),
        )
        for m in range(1, slabs)
    ]
    start(scatter)
    rest = [(c, h * (rows // 2), rows // 2) for c in range(2, chunks) for h in range(2)]
    for piece in rest[:1]:
        forward_all(*piece)
    total = share_last[own_at, :]
    for m in range(1, slabs):
        scatter[m - 1].wait_recv()
        total = total + parts_in[m]
    gathered[0, me] = total

    def gather(it):
        return [
            remote(gathered.at[it, me], gathered.at[it, me], all_send.at[it, m], all_recv.at[it, m], (sub, ahead(m)))
            for m in range(1, slabs)
        ]

    gather_first = gather(0)
    start(gather_first)
    for piece in rest[1:]:
        forward_all(*piece)
    for copy in gather_first:
        copy.wait_recv()

    def face(it):
        apart = gathered[it].reshape(width, width)
        jump = exact(exact(basis_y[...], apart), x_t[...])
        modes = exact(exact(y_t[...], jump), basis_x[...]) * stiff_t[...]
        search = exact(exact(basis_y[...], modes), x_t[...]) * weight
        jump_t[...] = jump
        search_t[it] = search
        both = jnp.sum(jump * search, axis=(0, 1), keepdims=True)
        norm = jnp.sum(search * search, axis=(0, 1), keepdims=True)
        line = lax.broadcasted_iota(jnp.int32, (TILE, LANES), 0)
        sums_out[it] = jnp.where(line == 0, both, norm)

    def sums(it):
        return [
            remote(
                sums_out.at[it], sums_in.at[it, m], sum_send.at[it, m], sum_recv.at[it, m],
                (lax.rem(sub + m, subs), me),
            )
            for m in range(1, subs)
        ]

    def step_length(it, copies):
        total = sums_out[it]
        for m in range(1, subs):
            copies[m - 1].wait_recv()
            total = total + sums_in[it, m]
        return total[0:1, 0:1] / (total[1:2, 0:1] + 1e-06)

    face(0)
    sums_first = sums(0)
    start(sums_first)
    pass_on = remote(search_t.at[0], search_in, side_send.at[1], side_recv.at[1], (next_sub, me))
    pass_on.start()
    alpha = step_length(0, sums_first)
    mult_t[...] = alpha * search_t[0]
    force[1] = exact(exact(y_t[...], -mult_t[...]), basis_x[...]).T
    pass_on.wait_recv()
    force[0] = exact(exact(y_t[...], alpha * search_in[...]), basis_x[...]).T

    edge[...] = jnp.zeros_like(edge)

    def modal(c):
        def one(at, carry):
            mine = c * TILE + at
            j = me * rows + mine
            line = jnp.concatenate([line_of(lines, c * slabs + d, at) for d in range(slabs)], axis=0)
            hat = dot(xt_left[...], as_right(line))
            lane = lax.broadcasted_iota(jnp.int32, (width, width), 1)
            pick = lambda p: jnp.sum(jnp.where(lane == j, force[p], 0.0), axis=1, keepdims=True)
            hat = hat + pick(0) * basis_z[0:1, :] + pick(1) * basis_z[width - 1 : width, :]
            modes = hat / ((x_column[...] + yz_eigen[pl.ds(j, 1), :]) * own_rho)
            back = dot(x_left[...], as_right(modes))
            for h in range(halves):
                at_x = pl.ds(pl.multiple_of((h * TILE + at) * rows, TILE), rows)
                part = back[:, h * lanes : (h + 1) * lanes]
                spread[pl.ds(c * slabs, slabs), at_x, :] = part.reshape(slabs, rows, lanes)
            lane = lax.broadcasted_iota(jnp.int32, (width, LANES), 1)
            first = jnp.sum(modes * basis_z[0:1, :], axis=1, keepdims=True)
            last = jnp.sum(modes * basis_z[width - 1 : width, :], axis=1, keepdims=True)
            edge[...] += jnp.where(lane == mine, first, 0.0) + jnp.where(lane == rows + mine, last, 0.0)
            return carry

        for m in range(1, slabs):
            d = behind(m)
            remote(
                sent.at[d * chunks + c], lines.at[c * slabs + d], fwd_send.at[c, m], fwd_recv.at[c, m], (sub, d)
            ).wait_recv()
        keep(c).wait()
        lax.fori_loop(0, TILE, one, 0)

    def inverse(c):
        return [
            remote(
                spread.at[c * slabs + ahead(m)], got.at[c * slabs + me],
                inv_send.at[c, m], inv_recv.at[c, m], (sub, ahead(m)),
            )
            for m in range(1, slabs)
        ]

    back = [inverse(c) for c in range(chunks)]
    stay = lambda c: pltpu.make_async_copy(spread.at[c * slabs + me], got.at[c * slabs + me], own_sem.at[c])
    early = max(chunks // 2, 1)
    for c in range(chunks):
        modal(c)
        stay(c).start()
        if c < early:
            start(back[c])

    edge_t = edge[...].T
    ends_in[0] = edge_t[:rows]
    send_ends = remote(ends_in.at[0], ends_in.at[1], side_send.at[2], side_recv.at[2], (last_sub, me))
    send_ends.start()
    send_ends.wait_recv()
    gathered[1, me] = edge_t[rows : 2 * rows] - ends_in[1]
    gather_last = gather(1)
    start(gather_last)
    for c in range(early, chunks):
        start(back[c])

    write = lambda c: pltpu.make_async_copy(
        got.at[pl.ds(c * slabs, slabs)], fields.at[pl.ds(c * slabs, slabs)], out_sem.at[c]
    )

    def arrive(c):
        stay(c).wait()
        for m in range(1, slabs):
            d = behind(m)
            remote(
                spread.at[c * slabs + d], got.at[c * slabs + d], inv_send.at[c, m], inv_recv.at[c, m], (sub, d)
            ).wait_recv()

        def one(d, carry):
            at = [pl.ds(h * TILE * rows, TILE * rows) for h in range(halves)]
            whole = jnp.concatenate([got[c * slabs + d, at[h], :] for h in range(halves)], axis=1)
            whole = dot(as_left(whole), zt_right[...])
            for h in range(halves):
                got[c * slabs + d, at[h], :] = whole[:, h * lanes : (h + 1) * lanes]
            return carry

        lax.fori_loop(0, slabs, one, 0)
        write(c).start()

    for c in range(early):
        arrive(c)

    for copy in gather_last:
        copy.wait_recv()
    face(1)
    sums_last = sums(1)
    start(sums_last)
    alpha = step_length(1, sums_last)
    mult_t[...] = (mult_t[...] + alpha * search_t[1]).T
    own_mult[...] = mult_t[own_at, :]
    jump_t[...] = jump_t[...].T
    own_jump[...] = jump_t[own_at, :]

    for copies in (scatter, gather_first, gather_last, sums_first, sums_last, [pass_on, send_ends]):
        for copy in copies:
            copy.wait_send()
    for c in range(chunks):
        for m in range(1, slabs):
            forward(m, c, 0, rows).wait_send()

    for c in range(early, chunks):
        arrive(c)
    for c in range(chunks):
        write(c).wait()
        for copy in back[c]:
            copy.wait_send()


def as_right_first(value):
    top, low = split(value)
    return jnp.concatenate([top, top, low], axis=0)


def iterate(subs, slabs, source, coarse, rho, basis_x, basis_y, basis_z, eigen_x, eigen_y, eigen_z, stiff):
    rows, width = source.shape[1:3]
    chunks = rows // TILE
    face = lambda *lead: pltpu.VMEM((*lead, width, width), F32)
    lot = lambda *lead: pltpu.VMEM((*lead, rows, width), F32)
    lanes = min(width, LANES)
    block = (chunks * slabs, TILE * rows * (width // lanes), lanes)
    field = lambda: pltpu.VMEM(block, F32)
    dma = pltpu.SemaphoreType.DMA
    vmem = pl.BlockSpec(memory_space=pltpu.VMEM)
    hbm = pl.BlockSpec(memory_space=pl.ANY)
    return pl.pallas_call(
        functools.partial(feti_kernel, subs, slabs, rows, width),
        out_shape=(
            jax.ShapeDtypeStruct(block, F32),
            jax.ShapeDtypeStruct((rows, width), F32),
            jax.ShapeDtypeStruct((rows, width), F32),
        ),
        in_specs=[hbm, hbm, pl.BlockSpec(memory_space=pltpu.SMEM)] + [vmem] * 7,
        out_specs=(hbm, vmem, vmem),
        scratch_shapes=[
            face(2, GROUP), face(2, GROUP), field(), field(), field(), field(),
            pltpu.VMEM((3 * width, width), BF16), pltpu.VMEM((3 * width, width), BF16),
            pltpu.VMEM((width, 3 * width), BF16), pltpu.VMEM((width, 3 * width), BF16),
            pltpu.VMEM((width, 3 * width), BF16), face(), face(), face(),
            face(), face(), face(), face(), face(), face(),
            face(), face(), face(), lot(slabs), lot(ITERS, slabs), lot(2),
            face(), face(ITERS), face(), face(), face(2), pltpu.VMEM((width, LANES), F32),
            pltpu.VMEM((ITERS, TILE, LANES), F32), pltpu.VMEM((ITERS, subs, TILE, LANES), F32),
            dma((2, 2)), dma((chunks,)), dma((chunks,)),
            dma((chunks, slabs)), dma((chunks, slabs)), dma((chunks, slabs)), dma((chunks, slabs)),
            dma((slabs,)), dma((slabs,)), dma((ITERS, slabs)), dma((ITERS, slabs)),
            dma((3,)), dma((3,)), dma((ITERS, subs)), dma((ITERS, subs)),
        ],
        compiler_params=pltpu.CompilerParams(
            collective_id=0, has_side_effects=True, vmem_limit_bytes=60 * 2**20
        ),
        name="feti",
    )(source, coarse, rho, basis_x, basis_y, basis_z, eigen_x, eigen_y, eigen_z, stiff)


def last_kernel(field_ref, basis_ref, out_ref):
    left = as_left(basis_ref[...])
    blocks, halves, lot, count, lanes = field_ref.shape
    for at in range(count):
        parts = [field_ref[:, h, :, at, :].reshape(blocks * lot, lanes) for h in range(halves)]
        out_ref[at] = dot(left, as_right(jnp.concatenate(parts, axis=1)))


def last_product(fields, basis_y):
    blocks, halves, lot, rows, lanes = fields.shape
    width = basis_y.shape[0]
    return pl.pallas_call(
        last_kernel,
        out_shape=jax.ShapeDtypeStruct((rows, width, halves * lanes), F32),
        grid=(rows // TILE,),
        in_specs=[
            pl.BlockSpec((blocks, halves, lot, TILE, lanes), lambda x: (0, 0, 0, x, 0)),
            pl.BlockSpec((width, width), lambda x: (0, 0)),
        ],
        out_specs=pl.BlockSpec((TILE, width, halves * lanes), lambda x: (x, 0, 0)),
        compiler_params=pltpu.CompilerParams(vmem_limit_bytes=24 * 2**20),
        name="last_product",
    )(fields, basis_y)


def on_device(
    source, coarse, rho, basis_x, basis_y, basis_z, eigen_x, eigen_y, eigen_z, face_stiff
):
    subs = lax.axis_size("sub")
    slabs = lax.axis_size("slab")
    rows, width = source.shape[1:3]
    fields, multipliers, jump = iterate(
        subs, slabs, source, coarse, rho, basis_x, basis_y, basis_z,
        eigen_x[None], eigen_y[None], eigen_z[None], face_stiff,
    )
    chunks = rows // TILE
    turned = basis_y.reshape(width, slabs, chunks, TILE).swapaxes(1, 2).reshape(width, width)
    lanes = min(width, LANES)
    fields = fields.reshape(chunks * slabs, width // lanes, TILE, rows, lanes)
    solution = last_product(fields, turned)
    return (solution[None], multipliers[None], jump[None])


def solution(mesh):
    in_specs = (
        P("sub", "slab", None, None),
        P(None, "sub", "slab", None, None),
        P(),
        P(),
        P(),
        P(),
        P(),
        P(),
        P(),
        P(),
    )
    out_specs = (P("sub", "slab", None, None), P("sub", "slab", None), P("sub", "slab", None))
    return jax.shard_map(
        on_device, mesh=mesh, in_specs=in_specs, out_specs=out_specs, check_vma=False
    )
```

```python
import functools

import jax
import jax.numpy as jnp
from jax import lax
from jax.experimental import pallas as pl
from jax.experimental.pallas import tpu as pltpu
from jax.sharding import PartitionSpec as P

ITERS = 2
GROUP = 4
TILE = 8
LANES = 128

HI = lax.Precision.HIGHEST
F32 = jnp.float32
BF16 = jnp.bfloat16
MESH = pl.DeviceIdType.MESH


def split(value):
    top = value.astype(BF16)
    return top, (value - top.astype(F32)).astype(BF16)


def as_left(value):
    top, low = split(value)
    return jnp.concatenate([top, top, low], axis=1)


def as_right(value):
    top, low = split(value)
    return jnp.concatenate([top, low, top], axis=0)


def dot(left, right):
    return jnp.dot(left, right, preferred_element_type=F32)


def exact(left, right):
    return jnp.dot(left, right, preferred_element_type=F32, precision=HI)


def feti_kernel(
    subs, slabs, rows, width,
    source, coarse, rho, basis_x, basis_y, basis_z, eigen_x, eigen_y, eigen_z, stiff,
    solved, own_mult, own_jump,
    source_in, coarse_in, sent, lines, spread, got,
    z_right, zt_right, yt_left, xt_left, x_left, x_t, y_t, stiff_t,
    pair_eigen, yz_eigen, x_column, z_column, first_column, last_column,
    y_parts, share_first, share_last, beside, parts_in, half_sum, gathered, gathered_last, ends_in,
    jump_t, search_t, search_in, mult_t, force, edge, sums_out, sums_in,
    in_sem, own_sem, fwd_send, fwd_recv, inv_send, inv_recv, last_send, last_recv,
    part_send, part_recv, mirror_send, mirror_recv, all_send, all_recv, side_send, side_recv, sum_send, sum_recv,
):
    me = lax.axis_index("slab")
    sub = lax.axis_index("sub")
    chunks = rows // TILE
    lanes = min(width, LANES)
    halves = width // lanes
    step_rows = TILE * halves
    ahead = lambda m: lax.rem(me + m, slabs)
    behind = lambda m: lax.rem(me + slabs - m, slabs)
    half = slabs // 2
    block = lax.rem(me, half)
    side = me - block
    mirror = lax.rem(me + half, slabs)
    peer = lambda m: lax.rem(block + m, half)
    next_sub = lax.rem(sub + 1, subs)
    last_sub = lax.rem(sub + subs - 1, subs)
    own_rho = rho[sub]
    weight = 0.5 * (own_rho + rho[next_sub])

    def remote(src, dst, send, recv, target):
        return pltpu.make_async_remote_copy(
            src_ref=src, dst_ref=dst, send_sem=send, recv_sem=recv, device_id=target, device_id_type=MESH
        )

    def fetch(which, g, slot):
        at = pl.ds(g * GROUP, GROUP)
        return (
            pltpu.make_async_copy(source.at[0, at], source_in.at[slot], in_sem.at[0, slot]),
            pltpu.make_async_copy(coarse.at[which, 0, at], coarse_in.at[slot], in_sem.at[1, slot]),
        )

    def start(copies):
        for copy in copies:
            copy.start()

    start(fetch(1, 0, 0))

    barrier = pltpu.get_barrier_semaphore()
    for m in range(1, slabs):
        pl.semaphore_signal(barrier, inc=1, device_id=(sub, ahead(m)), device_id_type=MESH)
    for m in range(1, subs):
        pl.semaphore_signal(barrier, inc=1, device_id=(lax.rem(sub + m, subs), me), device_id_type=MESH)

    z_right[...] = as_right(basis_z[...])
    y_t[...] = basis_y[...].T
    yt_left[...] = as_left(y_t[...])

    pl.semaphore_wait(barrier, slabs + subs - 2)

    def forward(m, c, first, count):
        at = pl.ds(first * step_rows, count * step_rows)
        d = ahead(m)
        return remote(
            sent.at[d * chunks + c, at], lines.at[c * slabs + me, at],
            fwd_send.at[c, m], fwd_recv.at[c, m], (sub, d),
        )

    def forward_all(c, first, count):
        for m in range(1, slabs):
            forward(m, c, first, count).start()

    def transform(which, store, after):
        steps = rows // GROUP

        def step(g, carry):
            slot = lax.rem(g, 2)

            @pl.when(g + 1 < steps)
            def _():
                start(fetch(which, g + 1, 1 - slot))

            for copy in fetch(which, g, slot):
                copy.wait()
            for r in range(GROUP):
                load = source_in[slot, r] + coarse_in[slot, r]
                part = dot(as_left(load), z_right[...])
                part = dot(yt_left[...], as_right(part))
                for h in range(halves):
                    at = pl.ds(pl.multiple_of((g * GROUP + r) * step_rows + h * TILE, TILE), TILE)
                    store[:, at, :] = part[:, h * lanes : (h + 1) * lanes].reshape(width // TILE, TILE, lanes)
            after(g)
            return carry

        lax.fori_loop(0, steps, step, 0)

    transform(1, sent, lambda g: forward_all(0, g * GROUP, GROUP))
    if chunks > 1:
        forward_all(1, 0, rows)

    keep = lambda c: pltpu.make_async_copy(sent.at[me * chunks + c], lines.at[c * slabs + me], own_sem.at[c])
    for c in range(chunks):
        keep(c).start()

    start(fetch(0, 0, 0))
    square = lambda row: jnp.broadcast_to(row, (width, width))
    down = lambda row: square(row).T
    y_column = down(eigen_y[...])
    pair_eigen[...] = y_column + eigen_x[...]
    yz_eigen[...] = y_column + eigen_z[...]
    x_column[...] = down(eigen_x[...])
    z_column[...] = down(eigen_z[...])
    first_column[...] = down(basis_z[0:1, :])
    last_column[...] = down(basis_z[width - 1 : width, :])
    x_t[...] = basis_x[...].T
    xt_left[...] = as_left(x_t[...])
    x_left[...] = as_left(basis_x[...])
    zt_right[...] = as_right(basis_z[...].T)
    stiff_t[...] = stiff[...].T
    for c in range(chunks):
        own_y = jnp.concatenate([y_t[d * rows + c * TILE : d * rows + (c + 1) * TILE, :] for d in range(slabs)], axis=0)
        y_parts[c] = padded(own_y, True).T.astype(BF16)

    transform(0, spread, lambda g: None)
    quarter = rows // 4
    rest = [(c, q * quarter, quarter) for c in range(2, chunks) for q in range(4)]
    for piece in rest[:1]:
        forward_all(*piece)

    def line_of(ref, q, at):
        return jnp.concatenate(
            [ref[q, pl.ds(h * TILE + at, rows, stride=step_rows), :] for h in range(halves)], axis=1
        )

    own_x = as_right(basis_x[pl.ds(pl.multiple_of(me * rows, TILE), rows), :])

    def partial_edges(jg, carry):
        at_j = pl.ds(pl.multiple_of(jg * TILE, TILE), TILE)
        eigen = pair_eigen[at_j, :]
        firsts, lasts = [], []
        for at in range(TILE):
            left = as_right_first(line_of(spread, jg, at))
            hat = lax.dot_general(left, own_x, (((0,), (0,)), ((), ())), preferred_element_type=F32)
            modes = hat / (eigen[at : at + 1, :] + z_column[...])
            firsts.append(jnp.sum(modes * first_column[...], axis=0, keepdims=True))
            lasts.append(jnp.sum(modes * last_column[...], axis=0, keepdims=True))
        share_first[at_j, :] = jnp.concatenate(firsts, axis=0) / own_rho
        share_last[at_j, :] = jnp.concatenate(lasts, axis=0) / own_rho
        return carry

    lax.fori_loop(0, width // TILE, partial_edges, 0)

    aside = remote(share_first, beside, side_send.at[0], side_recv.at[0], (last_sub, me))
    aside.start()
    aside.wait()
    share_last[...] = share_last[...] - beside[...]

    own_at = pl.ds(pl.multiple_of(me * rows, TILE), rows)
    lot = width // half
    lot_at = lambda b: pl.ds(pl.multiple_of(b * lot, TILE), lot)
    scatter = [
        remote(share_last.at[lot_at(peer(m))], parts_in.at[m], part_send.at[m], part_recv.at[m], (sub, side + peer(m)))
        for m in range(1, half)
    ]
    start(scatter)
    for piece in rest[1:2]:
        forward_all(*piece)
    total = share_last[lot_at(block), :]
    for m in range(1, half):
        scatter[m - 1].wait_recv()
        total = total + parts_in[m]
    half_sum[...] = total
    swap = remote(half_sum, parts_in.at[0], mirror_send.at[0], mirror_recv.at[0], (sub, mirror))
    swap.start()
    for piece in rest[2:3]:
        forward_all(*piece)
    swap.wait_recv()
    gathered[lot_at(block), :] = total + parts_in[0]
    gather_first = [
        remote(
            gathered.at[lot_at(block)], gathered.at[lot_at(block)], all_send.at[0, m], all_recv.at[0, m],
            (sub, side + peer(m)),
        )
        for m in range(1, half)
    ]
    start(gather_first)
    for piece in rest[3:]:
        forward_all(*piece)
    for copy in gather_first:
        copy.wait_recv()

    def face(it, apart):
        jump = exact(exact(basis_y[...], apart), x_t[...])
        modes = exact(exact(y_t[...], jump), basis_x[...]) * stiff_t[...]
        search = exact(exact(basis_y[...], modes), x_t[...]) * weight
        jump_t[...] = jump
        search_t[it] = search
        both = jnp.sum(jump * search, axis=(0, 1), keepdims=True)
        norm = jnp.sum(search * search, axis=(0, 1), keepdims=True)
        line = lax.broadcasted_iota(jnp.int32, (TILE, LANES), 0)
        sums_out[it] = jnp.where(line == 0, both, norm)

    def sums(it):
        return [
            remote(
                sums_out.at[it], sums_in.at[it, m], sum_send.at[it, m], sum_recv.at[it, m],
                (lax.rem(sub + m, subs), me),
            )
            for m in range(1, subs)
        ]

    def step_length(it, copies):
        total = sums_out[it]
        for m in range(1, subs):
            copies[m - 1].wait_recv()
            total = total + sums_in[it, m]
        return total[0:1, 0:1] / (total[1:2, 0:1] + 1e-06)

    face(0, gathered[...])
    sums_first = sums(0)
    start(sums_first)
    pass_on = remote(search_t.at[0], search_in, side_send.at[1], side_recv.at[1], (next_sub, me))
    pass_on.start()
    alpha = step_length(0, sums_first)
    mult_t[...] = alpha * search_t[0]
    force[1] = exact(exact(y_t[...], -mult_t[...]), basis_x[...]).T
    pass_on.wait_recv()
    force[0] = exact(exact(y_t[...], alpha * search_in[...]), basis_x[...]).T

    edge[...] = jnp.zeros_like(edge)

    def modal(c):
        def one(at, carry):
            mine = c * TILE + at
            j = me * rows + mine
            line = jnp.concatenate([line_of(lines, c * slabs + d, at) for d in range(slabs)], axis=0)
            hat = dot(xt_left[...], as_right(line))
            lane = lax.broadcasted_iota(jnp.int32, (width, width), 1)
            pick = lambda p: jnp.sum(jnp.where(lane == j, force[p], 0.0), axis=1, keepdims=True)
            hat = hat + pick(0) * basis_z[0:1, :] + pick(1) * basis_z[width - 1 : width, :]
            modes = hat / ((x_column[...] + yz_eigen[pl.ds(j, 1), :]) * own_rho)
            back = dot(x_left[...], as_right(modes))
            for d in range(slabs):
                for h in range(halves):
                    at_x = pl.ds(h * TILE + at, rows, stride=step_rows)
                    spread[c * slabs + d, at_x, :] = back[d * rows : (d + 1) * rows, h * lanes : (h + 1) * lanes]
            lane = lax.broadcasted_iota(jnp.int32, (width, LANES), 1)
            first = jnp.sum(modes * basis_z[0:1, :], axis=1, keepdims=True)
            last = jnp.sum(modes * basis_z[width - 1 : width, :], axis=1, keepdims=True)
            edge[...] += jnp.where(lane == mine, first, 0.0) + jnp.where(lane == rows + mine, last, 0.0)
            return carry

        for m in range(1, slabs):
            d = behind(m)
            remote(
                sent.at[d * chunks + c], lines.at[c * slabs + d], fwd_send.at[c, m], fwd_recv.at[c, m], (sub, d)
            ).wait_recv()
        keep(c).wait()
        lax.fori_loop(0, TILE, one, 0)

    last = chunks - 1
    quarters = [pl.ds(q * quarter * step_rows, quarter * step_rows) for q in range(4)]

    def inverse(c, m, q=None):
        d = ahead(m)
        src, dst = spread.at[c * slabs + d], got.at[c * slabs + me]
        if q is None:
            return remote(src, dst, inv_send.at[c, m], inv_recv.at[c, m], (sub, d))
        return remote(src.at[quarters[q]], dst.at[quarters[q]], last_send.at[q, m], last_recv.at[q, m], (sub, d))

    def inverse_from(c, m, q=None):
        d = behind(m)
        src, dst = spread.at[c * slabs + d], got.at[c * slabs + d]
        if q is None:
            return remote(src, dst, inv_send.at[c, m], inv_recv.at[c, m], (sub, d))
        return remote(src.at[quarters[q]], dst.at[quarters[q]], last_send.at[q, m], last_recv.at[q, m], (sub, d))

    stay = lambda c: pltpu.make_async_copy(spread.at[c * slabs + me], got.at[c * slabs + me], own_sem.at[c])
    back = []

    def give(c):
        copies = [inverse(c, m, q) for q in (range(4) if c == last else [None]) for m in range(1, slabs)]
        start(copies)
        back.extend(copies)

    for c in range(chunks):
        modal(c)
        stay(c).start()
        if c == 0 and last > 0:
            give(c)

    edge_t = edge[...].T
    ends_in[0] = edge_t[:rows]
    send_ends = remote(ends_in.at[0], ends_in.at[1], side_send.at[2], side_recv.at[2], (last_sub, me))
    send_ends.start()
    send_ends.wait_recv()
    gathered_last[own_at, :] = edge_t[rows : 2 * rows] - ends_in[1]
    far_at = pl.ds(pl.multiple_of(mirror * rows, TILE), rows)

    def hand(at, k, m, target):
        return remote(gathered_last.at[at], gathered_last.at[at], all_send.at[k, m], all_recv.at[k, m], (sub, target))

    swap_last = remote(
        gathered_last.at[own_at], gathered_last.at[own_at], mirror_send.at[1], mirror_recv.at[1], (sub, mirror)
    )
    swap_last.start()
    gather_own = [hand(own_at, 1, m, side + peer(m)) for m in range(1, half)]
    gather_far = [hand(far_at, 2, m, side + peer(m)) for m in range(1, half)]
    start(gather_own)
    for c in range(1, min(2, last)):
        give(c)

    def finish(c, q):
        def depth(d, carry):
            whole = got[c * slabs + d, quarters_at(q), :].reshape(quarter, halves, TILE, lanes)
            whole = jnp.concatenate([whole[:, h].reshape(quarter * TILE, lanes) for h in range(halves)], axis=1)
            whole = dot(as_left(whole), zt_right[...])
            whole = [whole[:, h * lanes : (h + 1) * lanes].reshape(quarter, 1, TILE, lanes) for h in range(halves)]
            got[c * slabs + d, quarters_at(q), :] = jnp.concatenate(whole, axis=1).reshape(quarter * step_rows, lanes)
            return carry

        lax.fori_loop(0, slabs, depth, 0)

        def across(r, carry):
            x = q * quarter + r
            at = [pl.ds(pl.multiple_of(x * step_rows + h * TILE, TILE), TILE) for h in range(halves)]
            right = jnp.concatenate(
                [
                    jnp.concatenate([got[c * slabs + d, at[h], :] for d in range(slabs)], axis=0)
                    for h in range(halves)
                ],
                axis=1,
            )
            part = dot(y_parts[c], padded(right, False).astype(BF16))
            solved[x] = part if c == 0 else solved[x] + part
            return carry

        lax.fori_loop(0, quarter, across, 0)

    quarters_at = lambda q: pl.ds(pl.multiple_of(q * quarter * step_rows, TILE), quarter * step_rows)

    def arrive(c):
        stay(c).wait()
        if c < last:
            for m in range(1, slabs):
                inverse_from(c, m).wait_recv()

            def one(q, carry):
                finish(c, q)
                return carry

            lax.fori_loop(0, 4, one, 0)
        else:
            for q in range(4):
                for m in range(1, slabs):
                    inverse_from(c, m, q).wait_recv()
                finish(c, q)

    if last > 0:
        arrive(0)
    swap_last.wait_recv()
    start(gather_far)
    for c in range(min(2, last), chunks):
        give(c)
    for c in range(1, last - 1):
        arrive(c)
    for copy in gather_own + gather_far:
        copy.wait_recv()
    face(1, gathered_last[...])
    sums_last = sums(1)
    start(sums_last)
    alpha = step_length(1, sums_last)
    mult_t[...] = (mult_t[...] + alpha * search_t[1]).T
    own_mult[...] = mult_t[own_at, :]
    jump_t[...] = jump_t[...].T
    own_jump[...] = jump_t[own_at, :]

    small = [scatter, [swap, swap_last, pass_on, send_ends], gather_first, gather_own, gather_far, sums_first, sums_last]
    for copies in small:
        for copy in copies:
            copy.wait_send()
    for c in range(chunks):
        for m in range(1, slabs):
            forward(m, c, 0, rows).wait_send()

    for c in range(max(1, last - 1) if last else 0, chunks):
        arrive(c)
    for copy in back:
        copy.wait_send()


def padded(value, left):
    top = value.astype(BF16).astype(F32)
    low = value - top
    parts = [top, top, low] if left else [top, low, top]
    over = -3 * value.shape[0] % LANES
    if over:
        parts.append(jnp.zeros((over, value.shape[1]), F32))
    return jnp.concatenate(parts, axis=0)


def as_right_first(value):
    top, low = split(value)
    return jnp.concatenate([top, top, low], axis=0)


def iterate(subs, slabs, source, coarse, rho, basis_x, basis_y, basis_z, eigen_x, eigen_y, eigen_z, stiff):
    rows, width = source.shape[1:3]
    chunks = rows // TILE
    face = lambda *lead: pltpu.VMEM((*lead, width, width), F32)
    lot = lambda *lead: pltpu.VMEM((*lead, rows, width), F32)
    lanes = min(width, LANES)
    field = lambda: pltpu.VMEM((chunks * slabs, TILE * rows * (width // lanes), lanes), F32)
    half = slabs // 2
    stack = 3 * slabs * TILE
    stack += -stack % LANES
    dma = pltpu.SemaphoreType.DMA
    vmem = pl.BlockSpec(memory_space=pltpu.VMEM)
    hbm = pl.BlockSpec(memory_space=pl.ANY)
    return pl.pallas_call(
        functools.partial(feti_kernel, subs, slabs, rows, width),
        out_shape=(
            pltpu.VMEM((rows, width, width), F32),
            pltpu.VMEM((rows, width), F32),
            pltpu.VMEM((rows, width), F32),
        ),
        in_specs=[hbm, hbm, pl.BlockSpec(memory_space=pltpu.SMEM)] + [vmem] * 7,
        out_specs=(vmem, vmem, vmem),
        scratch_shapes=[
            face(2, GROUP), face(2, GROUP), field(), field(), field(), field(),
            pltpu.VMEM((3 * width, width), BF16), pltpu.VMEM((3 * width, width), BF16),
            pltpu.VMEM((width, 3 * width), BF16), pltpu.VMEM((width, 3 * width), BF16),
            pltpu.VMEM((width, 3 * width), BF16), face(), face(), face(),
            face(), face(), face(), face(), face(), face(),
            pltpu.VMEM((chunks, width, stack), BF16),
            face(), face(), face(), pltpu.VMEM((half, width // half, width), F32),
            pltpu.VMEM((width // half, width), F32), face(), face(), lot(2),
            face(), face(ITERS), face(), face(), face(2), pltpu.VMEM((width, LANES), F32),
            pltpu.VMEM((ITERS, TILE, LANES), F32), pltpu.VMEM((ITERS, subs, TILE, LANES), F32),
            dma((2, 2)), dma((chunks,)),
            dma((chunks, slabs)), dma((chunks, slabs)), dma((chunks, slabs)), dma((chunks, slabs)),
            dma((4, slabs)), dma((4, slabs)),
            dma((half,)), dma((half,)), dma((2,)), dma((2,)), dma((3, half)), dma((3, half)),
            dma((3,)), dma((3,)), dma((ITERS, subs)), dma((ITERS, subs)),
        ],
        compiler_params=pltpu.CompilerParams(
            collective_id=0, has_side_effects=True, vmem_limit_bytes=54 * 2**20
        ),
        name="feti",
    )(source, coarse, rho, basis_x, basis_y, basis_z, eigen_x, eigen_y, eigen_z, stiff)


def on_device(
    source, coarse, rho, basis_x, basis_y, basis_z, eigen_x, eigen_y, eigen_z, face_stiff
):
    subs = lax.axis_size("sub")
    slabs = lax.axis_size("slab")
    solved, multipliers, jump = iterate(
        subs, slabs, source, coarse, rho, basis_x, basis_y, basis_z,
        eigen_x[None], eigen_y[None], eigen_z[None], face_stiff,
    )
    return (solved[None], multipliers[None], jump[None])


def solution(mesh):
    in_specs = (
        P("sub", "slab", None, None),
        P(None, "sub", "slab", None, None),
        P(),
        P(),
        P(),
        P(),
        P(),
        P(),
        P(),
        P(),
    )
    out_specs = (P("sub", "slab", None, None), P("sub", "slab", None), P("sub", "slab", None))
    return jax.shard_map(
        on_device, mesh=mesh, in_specs=in_specs, out_specs=out_specs, check_vma=False
    )
```

```python
import functools

import jax
import jax.numpy as jnp
from jax import lax
from jax.experimental import pallas as pl
from jax.experimental.pallas import tpu as pltpu
from jax.sharding import PartitionSpec as P

ITERS = 2
GROUP = 2
PIECES = 8
HAND_OUT = 8
TILE = 8
LANES = 128

HI = lax.Precision.HIGHEST
F32 = jnp.float32
BF16 = jnp.bfloat16
MESH = pl.DeviceIdType.MESH


def split(value):
    top = value.astype(BF16)
    return top, (value - top.astype(F32)).astype(BF16)


def as_left(value):
    top, low = split(value)
    return jnp.concatenate([top, top, low], axis=1)


def as_right(value):
    top, low = split(value)
    return jnp.concatenate([top, low, top], axis=0)


def dot(left, right):
    return jnp.dot(left, right, preferred_element_type=F32)


def exact(left, right):
    return jnp.dot(left, right, preferred_element_type=F32, precision=HI)


def feti_kernel(
    subs, slabs, rows, width,
    source, coarse, rho, *refs,
):
    tables, kept = refs[:7], refs[10:17]
    copies = [pltpu.make_async_copy(a, b, refs[17].at[i]) for i, (a, b) in enumerate(zip(tables, kept))]
    run(subs, slabs, rows, width, source, coarse, rho, copies, *kept, *refs[7:10], *refs[18:])


def run(
    subs, slabs, rows, width, source, coarse, rho, copies,
    basis_x, basis_y, basis_z, eigen_x, eigen_y, eigen_z, stiff,
    solved, own_mult, own_jump,
    source_in, coarse_in, sent, lines, spread, got,
    z_right, zt_right, yt_left, xt_left, x_left, x_t, y_t, stiff_t,
    pair_eigen, yz_eigen, x_column, z_column, first_column, last_column,
    y_parts, share_first, share_last, beside, parts_in, half_sum, gathered, gathered_last, ends_in,
    jump_t, search_t, search_in, mult_t, force, edge, sums_out, sums_in,
    in_sem, own_sem, fwd_send, fwd_recv, inv_send, inv_recv, last_send, last_recv,
    part_send, part_recv, mirror_send, mirror_recv, all_send, all_recv, side_send, side_recv, sum_send, sum_recv,
):
    me = lax.axis_index("slab")
    sub = lax.axis_index("sub")
    chunks = rows // TILE
    lanes = min(width, LANES)
    halves = width // lanes
    step_rows = TILE * halves
    ahead = lambda m: lax.rem(me + m, slabs)
    behind = lambda m: lax.rem(me + slabs - m, slabs)
    half = slabs // 2
    block = lax.rem(me, half)
    side = me - block
    mirror = lax.rem(me + half, slabs)
    peer = lambda m: lax.rem(block + m, half)
    next_sub = lax.rem(sub + 1, subs)
    last_sub = lax.rem(sub + subs - 1, subs)
    own_rho = rho[sub]
    weight = 0.5 * (own_rho + rho[next_sub])

    def remote(src, dst, send, recv, target):
        return pltpu.make_async_remote_copy(
            src_ref=src, dst_ref=dst, send_sem=send, recv_sem=recv, device_id=target, device_id_type=MESH
        )

    def fetch(which, g, slot):
        at = pl.ds(g * GROUP, GROUP)
        return (
            pltpu.make_async_copy(source.at[0, at], source_in.at[slot], in_sem.at[0, slot]),
            pltpu.make_async_copy(coarse.at[which, 0, at], coarse_in.at[slot], in_sem.at[1, slot]),
        )

    def start(copies):
        for copy in copies:
            copy.start()

    start(fetch(1, 0, 0))
    start([copies[2], copies[1]])

    barrier = pltpu.get_barrier_semaphore()
    for m in range(1, slabs):
        pl.semaphore_signal(barrier, inc=1, device_id=(sub, ahead(m)), device_id_type=MESH)
    for m in range(1, subs):
        pl.semaphore_signal(barrier, inc=1, device_id=(lax.rem(sub + m, subs), me), device_id_type=MESH)

    start(copies[at] for at in (0, 3, 4, 5, 6))
    copies[2].wait()
    z_right[...] = as_right(basis_z[...])
    copies[1].wait()
    y_t[...] = basis_y[...].T
    yt_left[...] = as_left(y_t[...])

    pl.semaphore_wait(barrier, slabs + subs - 2)

    def forward(m, c, first, count):
        at = pl.ds(first * step_rows, count * step_rows)
        d = ahead(m)
        return remote(
            sent.at[d * chunks + c, at], lines.at[c * slabs + me, at],
            fwd_send.at[c, m], fwd_recv.at[c, m], (sub, d),
        )

    def forward_all(c, first, count):
        for m in range(1, slabs):
            forward(m, c, first, count).start()

    def transform(which, store, after):
        steps = rows // GROUP

        def step(g, carry):
            slot = lax.rem(g, 2)

            @pl.when(g + 1 < steps)
            def _():
                start(fetch(which, g + 1, 1 - slot))

            for copy in fetch(which, g, slot):
                copy.wait()
            for r in range(GROUP):
                load = source_in[slot, r] + coarse_in[slot, r]
                part = dot(as_left(load), z_right[...])
                part = dot(yt_left[...], as_right(part))
                for h in range(halves):
                    at = pl.ds(pl.multiple_of((g * GROUP + r) * step_rows + h * TILE, TILE), TILE)
                    store[:, at, :] = part[:, h * lanes : (h + 1) * lanes].reshape(width // TILE, TILE, lanes)
            after(g)
            return carry

        lax.fori_loop(0, steps, step, 0)

    transform(1, sent, lambda g: forward_all(0, g * GROUP, GROUP))
    if chunks > 1:
        forward_all(1, 0, rows)

    keep = lambda c: pltpu.make_async_copy(sent.at[me * chunks + c], lines.at[c * slabs + me], own_sem.at[c])
    for c in range(chunks):
        keep(c).start()

    start(fetch(0, 0, 0))
    for at in (0, 3, 4, 5, 6):
        copies[at].wait()
    square = lambda row: jnp.broadcast_to(row, (width, width))
    down = lambda row: square(row).T
    y_column = down(eigen_y[...])
    pair_eigen[...] = y_column + eigen_x[...]
    yz_eigen[...] = y_column + eigen_z[...]
    x_column[...] = down(eigen_x[...])
    z_column[...] = down(eigen_z[...])
    first_column[...] = down(basis_z[0:1, :])
    last_column[...] = down(basis_z[width - 1 : width, :])
    x_t[...] = basis_x[...].T
    xt_left[...] = as_left(x_t[...])
    x_left[...] = as_left(basis_x[...])
    zt_right[...] = as_right(basis_z[...].T)
    stiff_t[...] = stiff[...].T
    for c in range(chunks):
        own_y = jnp.concatenate([y_t[d * rows + c * TILE : d * rows + (c + 1) * TILE, :] for d in range(slabs)], axis=0)
        y_parts[c] = padded(own_y, True).T.astype(BF16)

    transform(0, spread, lambda g: None)
    rest = [(c, q * rows // 4, rows // 4) for c in range(2, chunks) for q in range(4)]
    for piece in rest[:1]:
        forward_all(*piece)

    def line_of(ref, q, at):
        return jnp.concatenate(
            [ref[q, pl.ds(h * TILE + at, rows, stride=step_rows), :] for h in range(halves)], axis=1
        )

    own_x = as_right(basis_x[pl.ds(pl.multiple_of(me * rows, TILE), rows), :])

    def partial_edges(jg, carry):
        at_j = pl.ds(pl.multiple_of(jg * TILE, TILE), TILE)
        eigen = pair_eigen[at_j, :]
        firsts, lasts = [], []
        for at in range(TILE):
            left = as_right_first(line_of(spread, jg, at))
            hat = lax.dot_general(left, own_x, (((0,), (0,)), ((), ())), preferred_element_type=F32)
            modes = hat / (eigen[at : at + 1, :] + z_column[...])
            firsts.append(jnp.sum(modes * first_column[...], axis=0, keepdims=True))
            lasts.append(jnp.sum(modes * last_column[...], axis=0, keepdims=True))
        share_first[at_j, :] = jnp.concatenate(firsts, axis=0) / own_rho
        share_last[at_j, :] = jnp.concatenate(lasts, axis=0) / own_rho
        return carry

    lax.fori_loop(0, width // TILE, partial_edges, 0)

    aside = remote(share_first, beside, side_send.at[0], side_recv.at[0], (last_sub, me))
    aside.start()
    aside.wait()
    share_last[...] = share_last[...] - beside[...]

    own_at = pl.ds(pl.multiple_of(me * rows, TILE), rows)
    lot = width // half
    lot_at = lambda b: pl.ds(pl.multiple_of(b * lot, TILE), lot)
    scatter = [
        remote(share_last.at[lot_at(peer(m))], parts_in.at[m], part_send.at[m], part_recv.at[m], (sub, side + peer(m)))
        for m in range(1, half)
    ]
    start(scatter)
    for piece in rest[1:2]:
        forward_all(*piece)
    total = share_last[lot_at(block), :]
    for m in range(1, half):
        scatter[m - 1].wait_recv()
        total = total + parts_in[m]
    half_sum[...] = total
    swap = remote(half_sum, parts_in.at[0], mirror_send.at[0], mirror_recv.at[0], (sub, mirror))
    swap.start()
    for piece in rest[2:3]:
        forward_all(*piece)
    swap.wait_recv()
    gathered[lot_at(block), :] = total + parts_in[0]
    gather_first = [
        remote(
            gathered.at[lot_at(block)], gathered.at[lot_at(block)], all_send.at[0, m], all_recv.at[0, m],
            (sub, side + peer(m)),
        )
        for m in range(1, half)
    ]
    start(gather_first)
    for piece in rest[3:]:
        forward_all(*piece)
    for copy in gather_first:
        copy.wait_recv()

    def face(it, apart):
        jump = exact(exact(basis_y[...], apart), x_t[...])
        modes = exact(exact(y_t[...], jump), basis_x[...]) * stiff_t[...]
        search = exact(exact(basis_y[...], modes), x_t[...]) * weight
        jump_t[...] = jump
        search_t[it] = search
        both = jnp.sum(jump * search, axis=(0, 1), keepdims=True)
        norm = jnp.sum(search * search, axis=(0, 1), keepdims=True)
        line = lax.broadcasted_iota(jnp.int32, (TILE, LANES), 0)
        sums_out[it] = jnp.where(line == 0, both, norm)

    def sums(it):
        return [
            remote(
                sums_out.at[it], sums_in.at[it, m], sum_send.at[it, m], sum_recv.at[it, m],
                (lax.rem(sub + m, subs), me),
            )
            for m in range(1, subs)
        ]

    def step_length(it, copies):
        total = sums_out[it]
        for m in range(1, subs):
            copies[m - 1].wait_recv()
            total = total + sums_in[it, m]
        return total[0:1, 0:1] / (total[1:2, 0:1] + 1e-06)

    face(0, gathered[...])
    sums_first = sums(0)
    start(sums_first)
    pass_on = remote(search_t.at[0], search_in, side_send.at[1], side_recv.at[1], (next_sub, me))
    pass_on.start()
    alpha = step_length(0, sums_first)
    mult_t[...] = alpha * search_t[0]
    force[1] = exact(exact(y_t[...], -mult_t[...]), basis_x[...]).T
    pass_on.wait_recv()
    force[0] = exact(exact(y_t[...], alpha * search_in[...]), basis_x[...]).T

    edge[...] = jnp.zeros_like(edge)

    def modal(c):
        def one(at, carry):
            mine = c * TILE + at
            j = me * rows + mine
            line = jnp.concatenate([line_of(lines, c * slabs + d, at) for d in range(slabs)], axis=0)
            hat = dot(xt_left[...], as_right(line))
            lane = lax.broadcasted_iota(jnp.int32, (width, width), 1)
            pick = lambda p: jnp.sum(jnp.where(lane == j, force[p], 0.0), axis=1, keepdims=True)
            hat = hat + pick(0) * basis_z[0:1, :] + pick(1) * basis_z[width - 1 : width, :]
            modes = hat / ((x_column[...] + yz_eigen[pl.ds(j, 1), :]) * own_rho)
            back = dot(x_left[...], as_right(modes))
            for d in range(slabs):
                for h in range(halves):
                    at_x = pl.ds(h * TILE + at, rows, stride=step_rows)
                    spread[c * slabs + d, at_x, :] = back[d * rows : (d + 1) * rows, h * lanes : (h + 1) * lanes]
            lane = lax.broadcasted_iota(jnp.int32, (width, LANES), 1)
            first = jnp.sum(modes * basis_z[0:1, :], axis=1, keepdims=True)
            last = jnp.sum(modes * basis_z[width - 1 : width, :], axis=1, keepdims=True)
            edge[...] += jnp.where(lane == mine, first, 0.0) + jnp.where(lane == rows + mine, last, 0.0)
            return carry

        for m in range(1, slabs):
            d = behind(m)
            remote(
                sent.at[d * chunks + c], lines.at[c * slabs + d], fwd_send.at[c, m], fwd_recv.at[c, m], (sub, d)
            ).wait_recv()
        keep(c).wait()
        lax.fori_loop(0, TILE, one, 0)

    last = chunks - 1
    pieces = PIECES
    quarter = rows // pieces
    quarters = [pl.ds(q * quarter * step_rows, quarter * step_rows) for q in range(pieces)]

    def inverse(c, m, q=None):
        d = ahead(m)
        src, dst = spread.at[c * slabs + d], got.at[c * slabs + me]
        if q is None:
            return remote(src, dst, inv_send.at[c, m], inv_recv.at[c, m], (sub, d))
        return remote(src.at[quarters[q]], dst.at[quarters[q]], last_send.at[q, m], last_recv.at[q, m], (sub, d))

    def inverse_from(c, m, q=None):
        d = behind(m)
        src, dst = spread.at[c * slabs + d], got.at[c * slabs + d]
        if q is None:
            return remote(src, dst, inv_send.at[c, m], inv_recv.at[c, m], (sub, d))
        return remote(src.at[quarters[q]], dst.at[quarters[q]], last_send.at[q, m], last_recv.at[q, m], (sub, d))

    stay = lambda c: pltpu.make_async_copy(spread.at[c * slabs + me], got.at[c * slabs + me], own_sem.at[c])
    back = []

    def give(c):
        copies = [inverse(c, m, q) for q in (range(pieces) if c == last else [None]) for m in range(1, slabs)]
        start(copies)
        back.extend(copies)

    for c in range(chunks):
        modal(c)
        stay(c).start()
        if c == 0 and last > 0:
            give(c)

    edge_t = edge[...].T
    ends_in[0] = edge_t[:rows]
    send_ends = remote(ends_in.at[0], ends_in.at[1], side_send.at[2], side_recv.at[2], (last_sub, me))
    send_ends.start()
    send_ends.wait_recv()
    gathered_last[own_at, :] = edge_t[rows : 2 * rows] - ends_in[1]
    far_at = pl.ds(pl.multiple_of(mirror * rows, TILE), rows)

    def hand(at, k, m, target):
        return remote(gathered_last.at[at], gathered_last.at[at], all_send.at[k, m], all_recv.at[k, m], (sub, target))

    swap_last = remote(
        gathered_last.at[own_at], gathered_last.at[own_at], mirror_send.at[1], mirror_recv.at[1], (sub, mirror)
    )
    swap_last.start()
    gather_own = [hand(own_at, 1, m, side + peer(m)) for m in range(1, half)]
    gather_far = [hand(far_at, 2, m, side + peer(m)) for m in range(1, half)]
    start(gather_own)
    for c in range(1, min(2, last)):
        give(c)

    def finish(c, q):
        at = pl.ds(pl.multiple_of(q * quarter * step_rows, TILE), quarter * step_rows)
        whole = got[pl.ds(c * slabs, slabs), at, :].reshape(slabs * quarter, halves, TILE, lanes)
        whole = [whole[:, h].reshape(slabs * quarter * TILE, lanes) for h in range(halves)]
        whole = dot(as_left(jnp.concatenate(whole, axis=1)), zt_right[...])
        whole = whole.reshape(slabs, quarter, TILE, width)
        for r in range(quarter):
            part = dot(y_parts[c], padded(whole[:, r].reshape(slabs * TILE, width), False).astype(BF16))
            x = q * quarter + r
            solved[x] = part if c == 0 else solved[x] + part

    def arrive(c):
        stay(c).wait()
        if c < last:
            for m in range(1, slabs):
                inverse_from(c, m).wait_recv()

            def one(q, carry):
                finish(c, q)
                return carry

            lax.fori_loop(0, pieces, one, 0)
        else:
            for q in range(pieces):
                for m in range(1, slabs):
                    inverse_from(c, m, q).wait_recv()
                finish(c, q)

    if last > 0:
        arrive(0)
    swap_last.wait_recv()
    start(gather_far)
    for c in range(min(2, last), chunks):
        give(c)
    for c in range(1, last - 1):
        arrive(c)
    for copy in gather_own + gather_far:
        copy.wait_recv()
    face(1, gathered_last[...])
    sums_last = sums(1)
    start(sums_last)
    alpha = step_length(1, sums_last)
    mult_t[...] = (mult_t[...] + alpha * search_t[1]).T
    own_mult[...] = mult_t[own_at, :]
    jump_t[...] = jump_t[...].T
    own_jump[...] = jump_t[own_at, :]

    small = [scatter, [swap, swap_last, pass_on, send_ends], gather_first, gather_own, gather_far, sums_first, sums_last]
    for copies in small:
        for copy in copies:
            copy.wait_send()
    for c in range(chunks):
        for m in range(1, slabs):
            forward(m, c, 0, rows).wait_send()

    for c in range(max(1, last - 1) if last else 0, chunks):
        arrive(c)
    for copy in back:
        copy.wait_send()


def padded(value, left):
    top = value.astype(BF16).astype(F32)
    low = value - top
    parts = [top, top, low] if left else [top, low, top]
    over = -3 * value.shape[0] % LANES
    if over:
        parts.append(jnp.zeros((over, value.shape[1]), F32))
    return jnp.concatenate(parts, axis=0)


def as_right_first(value):
    top, low = split(value)
    return jnp.concatenate([top, top, low], axis=0)


def iterate(subs, slabs, source, coarse, rho, basis_x, basis_y, basis_z, eigen_x, eigen_y, eigen_z, stiff):
    rows, width = source.shape[1:3]
    chunks = rows // TILE
    face = lambda *lead: pltpu.VMEM((*lead, width, width), F32)
    lot = lambda *lead: pltpu.VMEM((*lead, rows, width), F32)
    lanes = min(width, LANES)
    field = lambda: pltpu.VMEM((chunks * slabs, TILE * rows * (width // lanes), lanes), F32)
    half = slabs // 2
    stack = 3 * slabs * TILE
    stack += -stack % LANES
    line = pltpu.VMEM((1, width), F32)
    dma = pltpu.SemaphoreType.DMA
    vmem = pl.BlockSpec(memory_space=pltpu.VMEM)
    hbm = pl.BlockSpec(memory_space=pl.ANY)
    return pl.pallas_call(
        functools.partial(feti_kernel, subs, slabs, rows, width),
        out_shape=(
            pltpu.VMEM((rows, width, width), F32),
            pltpu.VMEM((rows, width), F32),
            pltpu.VMEM((rows, width), F32),
        ),
        in_specs=[hbm, hbm, pl.BlockSpec(memory_space=pltpu.SMEM)] + [hbm] * 7,
        out_specs=(vmem, vmem, vmem),
        scratch_shapes=[
            face(), face(), face(), line, line, line, face(), dma((7,)),
            face(2, GROUP), face(2, GROUP), field(), field(), field(), field(),
            pltpu.VMEM((3 * width, width), BF16), pltpu.VMEM((3 * width, width), BF16),
            pltpu.VMEM((width, 3 * width), BF16), pltpu.VMEM((width, 3 * width), BF16),
            pltpu.VMEM((width, 3 * width), BF16), face(), face(), face(),
            face(), face(), face(), face(), face(), face(),
            pltpu.VMEM((chunks, width, stack), BF16),
            face(), face(), face(), pltpu.VMEM((half, width // half, width), F32),
            pltpu.VMEM((width // half, width), F32), face(), face(), lot(2),
            face(), face(ITERS), face(), face(), face(2), pltpu.VMEM((width, LANES), F32),
            pltpu.VMEM((ITERS, TILE, LANES), F32), pltpu.VMEM((ITERS, subs, TILE, LANES), F32),
            dma((2, 2)), dma((chunks,)),
            dma((chunks, slabs)), dma((chunks, slabs)), dma((chunks, slabs)), dma((chunks, slabs)),
            dma((PIECES, slabs)), dma((PIECES, slabs)),
            dma((half,)), dma((half,)), dma((2,)), dma((2,)), dma((3, half)), dma((3, half)),
            dma((3,)), dma((3,)), dma((ITERS, subs)), dma((ITERS, subs)),
        ],
        compiler_params=pltpu.CompilerParams(
            collective_id=0, has_side_effects=True, vmem_limit_bytes=54 * 2**20
        ),
        name="feti",
    )(source, coarse, rho, basis_x, basis_y, basis_z, eigen_x, eigen_y, eigen_z, stiff)


def hand_out_kernel(*refs):
    count = len(refs) // 2
    copies = []
    for i in range(count):
        parts = min(HAND_OUT, refs[i].shape[0]) if i == 0 else 1
        lot = refs[i].shape[0] // parts
        for part in range(parts):
            at = pl.ds(part * lot, lot)
            copies.append(pltpu.make_async_copy(refs[i].at[at], refs[count + i].at[at], refs[-1].at[len(copies)]))
    for copy in copies:
        copy.start()
    for copy in copies:
        copy.wait()


def hand_out(*results):
    anywhere = pl.BlockSpec(memory_space=pl.ANY)
    return pl.pallas_call(
        hand_out_kernel,
        out_shape=[pltpu.HBM(value.shape, value.dtype) for value in results],
        in_specs=[anywhere] * len(results),
        out_specs=[anywhere] * len(results),
        scratch_shapes=[pltpu.SemaphoreType.DMA((HAND_OUT + len(results),))],
        compiler_params=pltpu.CompilerParams(vmem_limit_bytes=2**20),
        name="hand_out",
    )(*(pltpu.with_memory_space_constraint(value, pltpu.VMEM) for value in results))


def on_device(
    source, coarse, rho, basis_x, basis_y, basis_z, eigen_x, eigen_y, eigen_z, face_stiff
):
    subs = lax.axis_size("sub")
    slabs = lax.axis_size("slab")
    solved, multipliers, jump = iterate(
        subs, slabs, source, coarse, rho, basis_x, basis_y, basis_z,
        eigen_x[None], eigen_y[None], eigen_z[None], face_stiff,
    )
    solved, multipliers, jump = hand_out(solved, multipliers, jump)
    return (solved[None], multipliers[None], jump[None])


def solution(mesh):
    in_specs = (
        P("sub", "slab", None, None),
        P(None, "sub", "slab", None, None),
        P(),
        P(),
        P(),
        P(),
        P(),
        P(),
        P(),
        P(),
    )
    out_specs = (P("sub", "slab", None, None), P("sub", "slab", None), P("sub", "slab", None))
    return jax.shard_map(
        on_device, mesh=mesh, in_specs=in_specs, out_specs=out_specs, check_vma=False
    )
```

```python
import functools

import jax
import jax.numpy as jnp
from jax import lax
from jax.experimental import pallas as pl
from jax.experimental.pallas import tpu as pltpu
from jax.sharding import PartitionSpec as P

ITERS = 2
GROUP = 2
PIECES = 4
HAND_OUT = 8
TILE = 8
LANES = 128

HI = lax.Precision.HIGHEST
F32 = jnp.float32
BF16 = jnp.bfloat16
MESH = pl.DeviceIdType.MESH


def split(value):
    top = value.astype(BF16)
    return top, (value - top.astype(F32)).astype(BF16)


def as_left(value):
    top, low = split(value)
    return jnp.concatenate([top, top, low], axis=1)


def as_right(value):
    top, low = split(value)
    return jnp.concatenate([top, low, top], axis=0)


def dot(left, right):
    return jnp.dot(left, right, preferred_element_type=F32)


def exact(left, right):
    return jnp.dot(left, right, preferred_element_type=F32, precision=HI)


def feti_kernel(
    subs, slabs, rows, width,
    source, coarse, rho, *refs,
):
    tables, kept = refs[:7], refs[10:17]
    copies = [pltpu.make_async_copy(a, b, refs[17].at[i]) for i, (a, b) in enumerate(zip(tables, kept))]
    run(subs, slabs, rows, width, source, coarse, rho, copies, *kept, *refs[7:10], *refs[18:])


def run(
    subs, slabs, rows, width, source, coarse, rho, copies,
    basis_x, basis_y, basis_z, eigen_x, eigen_y, eigen_z, stiff,
    solved, own_mult, own_jump,
    source_in, coarse_in, sent, lines, spread, got,
    z_right, zt_right, yt_left, xt_left, x_left, x_t, y_t, stiff_t,
    pair_eigen, yz_eigen, x_column, z_column, first_column, last_column,
    y_parts, share_first, share_last, beside, parts_in, half_sum, gathered, gathered_last, ends_in,
    jump_t, search_t, search_in, mult_t, force, edge, sums_out, sums_in,
    in_sem, own_sem, fwd_send, fwd_recv, inv_send, inv_recv, last_send, last_recv,
    part_send, part_recv, mirror_send, mirror_recv, all_send, all_recv, side_send, side_recv, sum_send, sum_recv,
):
    me = lax.axis_index("slab")
    sub = lax.axis_index("sub")
    chunks = rows // TILE
    lanes = min(width, LANES)
    halves = width // lanes
    step_rows = TILE * halves
    ahead = lambda m: lax.rem(me + m, slabs)
    behind = lambda m: lax.rem(me + slabs - m, slabs)
    half = slabs // 2
    block = lax.rem(me, half)
    side = me - block
    mirror = lax.rem(me + half, slabs)
    peer = lambda m: lax.rem(block + m, half)
    next_sub = lax.rem(sub + 1, subs)
    last_sub = lax.rem(sub + subs - 1, subs)
    own_rho = rho[sub]
    weight = 0.5 * (own_rho + rho[next_sub])

    def remote(src, dst, send, recv, target):
        return pltpu.make_async_remote_copy(
            src_ref=src, dst_ref=dst, send_sem=send, recv_sem=recv, device_id=target, device_id_type=MESH
        )

    def fetch(which, g, slot):
        at = pl.ds(g * GROUP, GROUP)
        return (
            pltpu.make_async_copy(source.at[0, at], source_in.at[slot], in_sem.at[0, slot]),
            pltpu.make_async_copy(coarse.at[which, 0, at], coarse_in.at[slot], in_sem.at[1, slot]),
        )

    def start(copies):
        for copy in copies:
            copy.start()

    start(fetch(1, 0, 0))
    start([copies[2], copies[1]])

    barrier = pltpu.get_barrier_semaphore()
    for m in range(1, slabs):
        pl.semaphore_signal(barrier, inc=1, device_id=(sub, ahead(m)), device_id_type=MESH)
    for m in range(1, subs):
        pl.semaphore_signal(barrier, inc=1, device_id=(lax.rem(sub + m, subs), me), device_id_type=MESH)

    start(copies[at] for at in (0, 3, 4, 5, 6))
    copies[2].wait()
    z_right[...] = as_right(basis_z[...])
    copies[1].wait()
    y_t[...] = basis_y[...].T
    yt_left[...] = as_left(y_t[...])

    def forward(m, c, first, count):
        at = pl.ds(first * step_rows, count * step_rows)
        d = ahead(m)
        return remote(
            sent.at[d * chunks + c, at], lines.at[c * slabs + me, at],
            fwd_send.at[c, m], fwd_recv.at[c, m], (sub, d),
        )

    def forward_all(c, first, count):
        for m in range(1, slabs):
            forward(m, c, first, count).start()

    def transform(which, store):
        steps = rows // GROUP

        def step(g, carry):
            slot = lax.rem(g, 2)

            @pl.when(g + 1 < steps)
            def _():
                start(fetch(which, g + 1, 1 - slot))

            for copy in fetch(which, g, slot):
                copy.wait()
            for r in range(GROUP):
                load = source_in[slot, r] + coarse_in[slot, r]
                part = dot(as_left(load), z_right[...])
                part = dot(yt_left[...], as_right(part))
                for h in range(halves):
                    at = pl.ds(pl.multiple_of((g * GROUP + r) * step_rows + h * TILE, TILE), TILE)
                    store[:, at, :] = part[:, h * lanes : (h + 1) * lanes].reshape(width // TILE, TILE, lanes)
            return carry

        return steps, step

    steps, step = transform(1, sent)
    step(0, 0)
    pl.semaphore_wait(barrier, slabs + subs - 2)
    forward_all(0, 0, GROUP)

    def step_and_send(g, carry):
        step(g, carry)
        forward_all(0, g * GROUP, GROUP)
        return carry

    lax.fori_loop(1, steps, step_and_send, 0)
    if chunks > 1:
        forward_all(1, 0, rows)

    keep = lambda c: pltpu.make_async_copy(sent.at[me * chunks + c], lines.at[c * slabs + me], own_sem.at[c])
    for c in range(chunks):
        keep(c).start()

    start(fetch(0, 0, 0))
    for at in (0, 3, 4, 5, 6):
        copies[at].wait()
    square = lambda row: jnp.broadcast_to(row, (width, width))
    down = lambda row: square(row).T
    y_column = down(eigen_y[...])
    pair_eigen[...] = y_column + eigen_x[...]
    yz_eigen[...] = y_column + eigen_z[...]
    x_column[...] = down(eigen_x[...])
    z_column[...] = down(eigen_z[...])
    first_column[...] = down(basis_z[0:1, :])
    last_column[...] = down(basis_z[width - 1 : width, :])
    x_t[...] = basis_x[...].T
    xt_left[...] = as_left(x_t[...])
    x_left[...] = as_left(basis_x[...])
    zt_right[...] = as_right(basis_z[...].T)
    stiff_t[...] = stiff[...].T
    for c in range(chunks):
        own_y = jnp.concatenate([y_t[d * rows + c * TILE : d * rows + (c + 1) * TILE, :] for d in range(slabs)], axis=0)
        y_parts[c] = padded(own_y, True).T.astype(BF16)

    lax.fori_loop(0, *transform(0, spread), 0)
    rest = [(c, q * rows // 4, rows // 4) for c in range(2, chunks) for q in range(4)]
    for piece in rest[:1]:
        forward_all(*piece)

    def line_of(ref, q, at):
        return jnp.concatenate(
            [ref[q, pl.ds(h * TILE + at, rows, stride=step_rows), :] for h in range(halves)], axis=1
        )

    own_x = as_right(basis_x[pl.ds(pl.multiple_of(me * rows, TILE), rows), :])

    def partial_edges(jg, carry):
        at_j = pl.ds(pl.multiple_of(jg * TILE, TILE), TILE)
        eigen = pair_eigen[at_j, :]
        firsts, lasts = [], []
        for at in range(TILE):
            left = as_right_first(line_of(spread, jg, at))
            hat = lax.dot_general(left, own_x, (((0,), (0,)), ((), ())), preferred_element_type=F32)
            modes = hat / (eigen[at : at + 1, :] + z_column[...])
            firsts.append(jnp.sum(modes * first_column[...], axis=0, keepdims=True))
            lasts.append(jnp.sum(modes * last_column[...], axis=0, keepdims=True))
        share_first[at_j, :] = jnp.concatenate(firsts, axis=0) / own_rho
        share_last[at_j, :] = jnp.concatenate(lasts, axis=0) / own_rho
        return carry

    lax.fori_loop(0, width // TILE, partial_edges, 0)

    aside = remote(share_first, beside, side_send.at[0], side_recv.at[0], (last_sub, me))
    aside.start()
    aside.wait()
    share_last[...] = share_last[...] - beside[...]

    own_at = pl.ds(pl.multiple_of(me * rows, TILE), rows)
    lot = width // half
    lot_at = lambda b: pl.ds(pl.multiple_of(b * lot, TILE), lot)
    scatter = [
        remote(share_last.at[lot_at(peer(m))], parts_in.at[m], part_send.at[m], part_recv.at[m], (sub, side + peer(m)))
        for m in range(1, half)
    ]
    start(scatter)
    for piece in rest[1:2]:
        forward_all(*piece)
    total = share_last[lot_at(block), :]
    for m in range(1, half):
        scatter[m - 1].wait_recv()
        total = total + parts_in[m]
    half_sum[...] = total
    swap = remote(half_sum, parts_in.at[0], mirror_send.at[0], mirror_recv.at[0], (sub, mirror))
    swap.start()
    for piece in rest[2:3]:
        forward_all(*piece)
    swap.wait_recv()
    gathered[lot_at(block), :] = total + parts_in[0]
    gather_first = [
        remote(
            gathered.at[lot_at(block)], gathered.at[lot_at(block)], all_send.at[0, m], all_recv.at[0, m],
            (sub, side + peer(m)),
        )
        for m in range(1, half)
    ]
    start(gather_first)
    for piece in rest[3:]:
        forward_all(*piece)
    for copy in gather_first:
        copy.wait_recv()

    def face(it, apart):
        jump = exact(exact(basis_y[...], apart), x_t[...])
        modes = exact(exact(y_t[...], jump), basis_x[...]) * stiff_t[...]
        search = exact(exact(basis_y[...], modes), x_t[...]) * weight
        jump_t[...] = jump
        search_t[it] = search
        both = jnp.sum(jump * search, axis=(0, 1), keepdims=True)
        norm = jnp.sum(search * search, axis=(0, 1), keepdims=True)
        line = lax.broadcasted_iota(jnp.int32, (TILE, LANES), 0)
        sums_out[it] = jnp.where(line == 0, both, norm)

    def sums(it):
        return [
            remote(
                sums_out.at[it], sums_in.at[it, m], sum_send.at[it, m], sum_recv.at[it, m],
                (lax.rem(sub + m, subs), me),
            )
            for m in range(1, subs)
        ]

    def step_length(it, copies):
        total = sums_out[it]
        for m in range(1, subs):
            copies[m - 1].wait_recv()
            total = total + sums_in[it, m]
        return total[0:1, 0:1] / (total[1:2, 0:1] + 1e-06)

    face(0, gathered[...])
    sums_first = sums(0)
    start(sums_first)
    pass_on = remote(search_t.at[0], search_in, side_send.at[1], side_recv.at[1], (next_sub, me))
    pass_on.start()
    alpha = step_length(0, sums_first)
    mult_t[...] = alpha * search_t[0]
    force[1] = exact(exact(y_t[...], -mult_t[...]), basis_x[...]).T
    pass_on.wait_recv()
    force[0] = exact(exact(y_t[...], alpha * search_in[...]), basis_x[...]).T

    edge[...] = jnp.zeros_like(edge)

    def modal(c):
        def one(at, carry):
            mine = c * TILE + at
            j = me * rows + mine
            line = jnp.concatenate([line_of(lines, c * slabs + d, at) for d in range(slabs)], axis=0)
            hat = dot(xt_left[...], as_right(line))
            lane = lax.broadcasted_iota(jnp.int32, (width, width), 1)
            pick = lambda p: jnp.sum(jnp.where(lane == j, force[p], 0.0), axis=1, keepdims=True)
            hat = hat + pick(0) * basis_z[0:1, :] + pick(1) * basis_z[width - 1 : width, :]
            modes = hat / ((x_column[...] + yz_eigen[pl.ds(j, 1), :]) * own_rho)
            back = dot(x_left[...], as_right(modes))
            for d in range(slabs):
                for h in range(halves):
                    at_x = pl.ds(h * TILE + at, rows, stride=step_rows)
                    spread[c * slabs + d, at_x, :] = back[d * rows : (d + 1) * rows, h * lanes : (h + 1) * lanes]
            lane = lax.broadcasted_iota(jnp.int32, (width, LANES), 1)
            first = jnp.sum(modes * basis_z[0:1, :], axis=1, keepdims=True)
            last = jnp.sum(modes * basis_z[width - 1 : width, :], axis=1, keepdims=True)
            edge[...] += jnp.where(lane == mine, first, 0.0) + jnp.where(lane == rows + mine, last, 0.0)
            return carry

        for m in range(1, slabs):
            d = behind(m)
            remote(
                sent.at[d * chunks + c], lines.at[c * slabs + d], fwd_send.at[c, m], fwd_recv.at[c, m], (sub, d)
            ).wait_recv()
        keep(c).wait()
        lax.fori_loop(0, TILE, one, 0)

    last = chunks - 1
    pieces = PIECES
    quarter = rows // pieces
    quarters = [pl.ds(q * quarter * step_rows, quarter * step_rows) for q in range(pieces)]

    def inverse(c, m, q=None):
        d = ahead(m)
        src, dst = spread.at[c * slabs + d], got.at[c * slabs + me]
        if q is None:
            return remote(src, dst, inv_send.at[c, m], inv_recv.at[c, m], (sub, d))
        return remote(src.at[quarters[q]], dst.at[quarters[q]], last_send.at[q, m], last_recv.at[q, m], (sub, d))

    def inverse_from(c, m, q=None):
        d = behind(m)
        src, dst = spread.at[c * slabs + d], got.at[c * slabs + d]
        if q is None:
            return remote(src, dst, inv_send.at[c, m], inv_recv.at[c, m], (sub, d))
        return remote(src.at[quarters[q]], dst.at[quarters[q]], last_send.at[q, m], last_recv.at[q, m], (sub, d))

    stay = lambda c: pltpu.make_async_copy(spread.at[c * slabs + me], got.at[c * slabs + me], own_sem.at[c])
    back = []

    def give(c):
        copies = [inverse(c, m, q) for q in (range(pieces) if c == last else [None]) for m in range(1, slabs)]
        start(copies)
        back.extend(copies)

    for c in range(chunks):
        modal(c)
        stay(c).start()
        if c == 0 and last > 0:
            give(c)

    edge_t = edge[...].T
    ends_in[0] = edge_t[:rows]
    send_ends = remote(ends_in.at[0], ends_in.at[1], side_send.at[2], side_recv.at[2], (last_sub, me))
    send_ends.start()
    send_ends.wait_recv()
    gathered_last[own_at, :] = edge_t[rows : 2 * rows] - ends_in[1]
    far_at = pl.ds(pl.multiple_of(mirror * rows, TILE), rows)

    def hand(at, k, m, target):
        return remote(gathered_last.at[at], gathered_last.at[at], all_send.at[k, m], all_recv.at[k, m], (sub, target))

    swap_last = remote(
        gathered_last.at[own_at], gathered_last.at[own_at], mirror_send.at[1], mirror_recv.at[1], (sub, mirror)
    )
    swap_last.start()
    gather_own = [hand(own_at, 1, m, side + peer(m)) for m in range(1, half)]
    gather_far = [hand(far_at, 2, m, side + peer(m)) for m in range(1, half)]
    start(gather_own)
    for c in range(1, min(2, last)):
        give(c)

    def finish(c, q):
        at = pl.ds(pl.multiple_of(q * quarter * step_rows, TILE), quarter * step_rows)
        whole = got[pl.ds(c * slabs, slabs), at, :].reshape(slabs * quarter, halves, TILE, lanes)
        whole = [whole[:, h].reshape(slabs * quarter * TILE, lanes) for h in range(halves)]
        whole = dot(as_left(jnp.concatenate(whole, axis=1)), zt_right[...])
        whole = whole.reshape(slabs, quarter, TILE, width)
        for r in range(quarter):
            part = dot(y_parts[c], padded(whole[:, r].reshape(slabs * TILE, width), False).astype(BF16))
            x = q * quarter + r
            solved[x] = part if c == 0 else solved[x] + part

    def arrive(c):
        stay(c).wait()
        if c < last:
            for m in range(1, slabs):
                inverse_from(c, m).wait_recv()

            def one(q, carry):
                finish(c, q)
                return carry

            lax.fori_loop(0, pieces, one, 0)
        else:
            for q in range(pieces):
                for m in range(1, slabs):
                    inverse_from(c, m, q).wait_recv()
                finish(c, q)

    if last > 0:
        arrive(0)
    swap_last.wait_recv()
    start(gather_far)
    for c in range(min(2, last), chunks):
        give(c)
    for c in range(1, last - 1):
        arrive(c)
    for copy in gather_own + gather_far:
        copy.wait_recv()
    face(1, gathered_last[...])
    sums_last = sums(1)
    start(sums_last)
    alpha = step_length(1, sums_last)
    mult_t[...] = (mult_t[...] + alpha * search_t[1]).T
    own_mult[...] = mult_t[own_at, :]
    jump_t[...] = jump_t[...].T
    own_jump[...] = jump_t[own_at, :]

    small = [scatter, [swap, swap_last, pass_on, send_ends], gather_first, gather_own, gather_far, sums_first, sums_last]
    for copies in small:
        for copy in copies:
            copy.wait_send()
    for c in range(chunks):
        for m in range(1, slabs):
            forward(m, c, 0, rows).wait_send()

    for c in range(max(1, last - 1) if last else 0, chunks):
        arrive(c)
    for copy in back:
        copy.wait_send()


def padded(value, left):
    top = value.astype(BF16).astype(F32)
    low = value - top
    parts = [top, top, low] if left else [top, low, top]
    over = -3 * value.shape[0] % LANES
    if over:
        parts.append(jnp.zeros((over, value.shape[1]), F32))
    return jnp.concatenate(parts, axis=0)


def as_right_first(value):
    top, low = split(value)
    return jnp.concatenate([top, top, low], axis=0)


def iterate(subs, slabs, source, coarse, rho, basis_x, basis_y, basis_z, eigen_x, eigen_y, eigen_z, stiff):
    rows, width = source.shape[1:3]
    chunks = rows // TILE
    face = lambda *lead: pltpu.VMEM((*lead, width, width), F32)
    lot = lambda *lead: pltpu.VMEM((*lead, rows, width), F32)
    lanes = min(width, LANES)
    field = lambda: pltpu.VMEM((chunks * slabs, TILE * rows * (width // lanes), lanes), F32)
    half = slabs // 2
    stack = 3 * slabs * TILE
    stack += -stack % LANES
    line = pltpu.VMEM((1, width), F32)
    dma = pltpu.SemaphoreType.DMA
    vmem = pl.BlockSpec(memory_space=pltpu.VMEM)
    hbm = pl.BlockSpec(memory_space=pl.ANY)
    return pl.pallas_call(
        functools.partial(feti_kernel, subs, slabs, rows, width),
        out_shape=(
            pltpu.VMEM((rows, width, width), F32),
            pltpu.VMEM((rows, width), F32),
            pltpu.VMEM((rows, width), F32),
        ),
        in_specs=[hbm, hbm, pl.BlockSpec(memory_space=pltpu.SMEM)] + [hbm] * 7,
        out_specs=(vmem, vmem, vmem),
        scratch_shapes=[
            face(), face(), face(), line, line, line, face(), dma((7,)),
            face(2, GROUP), face(2, GROUP), field(), field(), field(), field(),
            pltpu.VMEM((3 * width, width), BF16), pltpu.VMEM((3 * width, width), BF16),
            pltpu.VMEM((width, 3 * width), BF16), pltpu.VMEM((width, 3 * width), BF16),
            pltpu.VMEM((width, 3 * width), BF16), face(), face(), face(),
            face(), face(), face(), face(), face(), face(),
            pltpu.VMEM((chunks, width, stack), BF16),
            face(), face(), face(), pltpu.VMEM((half, width // half, width), F32),
            pltpu.VMEM((width // half, width), F32), face(), face(), lot(2),
            face(), face(ITERS), face(), face(), face(2), pltpu.VMEM((width, LANES), F32),
            pltpu.VMEM((ITERS, TILE, LANES), F32), pltpu.VMEM((ITERS, subs, TILE, LANES), F32),
            dma((2, 2)), dma((chunks,)),
            dma((chunks, slabs)), dma((chunks, slabs)), dma((chunks, slabs)), dma((chunks, slabs)),
            dma((PIECES, slabs)), dma((PIECES, slabs)),
            dma((half,)), dma((half,)), dma((2,)), dma((2,)), dma((3, half)), dma((3, half)),
            dma((3,)), dma((3,)), dma((ITERS, subs)), dma((ITERS, subs)),
        ],
        compiler_params=pltpu.CompilerParams(
            collective_id=0, has_side_effects=True, vmem_limit_bytes=54 * 2**20
        ),
        name="feti",
    )(source, coarse, rho, basis_x, basis_y, basis_z, eigen_x, eigen_y, eigen_z, stiff)


def hand_out_kernel(*refs):
    count = len(refs) // 2
    copies = []
    for i in range(count):
        parts = min(HAND_OUT, refs[i].shape[0]) if i == 0 else 1
        lot = refs[i].shape[0] // parts
        for part in range(parts):
            at = pl.ds(part * lot, lot)
            copies.append(pltpu.make_async_copy(refs[i].at[at], refs[count + i].at[at], refs[-1].at[len(copies)]))
    for copy in copies:
        copy.start()
    for copy in copies:
        copy.wait()


def hand_out(*results):
    anywhere = pl.BlockSpec(memory_space=pl.ANY)
    return pl.pallas_call(
        hand_out_kernel,
        out_shape=[pltpu.HBM(value.shape, value.dtype) for value in results],
        in_specs=[anywhere] * len(results),
        out_specs=[anywhere] * len(results),
        scratch_shapes=[pltpu.SemaphoreType.DMA((HAND_OUT + len(results),))],
        compiler_params=pltpu.CompilerParams(vmem_limit_bytes=2**20),
        name="hand_out",
    )(*(pltpu.with_memory_space_constraint(value, pltpu.VMEM) for value in results))


def on_device(
    source, coarse, rho, basis_x, basis_y, basis_z, eigen_x, eigen_y, eigen_z, face_stiff
):
    subs = lax.axis_size("sub")
    slabs = lax.axis_size("slab")
    solved, multipliers, jump = iterate(
        subs, slabs, source, coarse, rho, basis_x, basis_y, basis_z,
        eigen_x[None], eigen_y[None], eigen_z[None], face_stiff,
    )
    solved, multipliers, jump = hand_out(solved, multipliers, jump)
    return (solved[None], multipliers[None], jump[None])


def solution(mesh):
    in_specs = (
        P("sub", "slab", None, None),
        P(None, "sub", "slab", None, None),
        P(),
        P(),
        P(),
        P(),
        P(),
        P(),
        P(),
        P(),
    )
    out_specs = (P("sub", "slab", None, None), P("sub", "slab", None), P("sub", "slab", None))
    return jax.shard_map(
        on_device, mesh=mesh, in_specs=in_specs, out_specs=out_specs, check_vma=False
    )
```

```python
import functools

import jax
import jax.numpy as jnp
from jax import lax
from jax.experimental import pallas as pl
from jax.experimental.pallas import tpu as pltpu
from jax.sharding import PartitionSpec as P

ITERS = 2
GROUP = 2
PIECES = 4
HAND_OUT = 8
TILE = 8
LANES = 128

HI = lax.Precision.HIGHEST
F32 = jnp.float32
BF16 = jnp.bfloat16
MESH = pl.DeviceIdType.MESH


def split(value):
    top = value.astype(BF16)
    return top, (value - top.astype(F32)).astype(BF16)


def as_left(value):
    top, low = split(value)
    return jnp.concatenate([top, top, low], axis=1)


def as_right(value):
    top, low = split(value)
    return jnp.concatenate([top, low, top], axis=0)


def dot(left, right):
    return jnp.dot(left, right, preferred_element_type=F32)


def exact(left, right):
    return jnp.dot(left, right, preferred_element_type=F32, precision=HI)


def feti_kernel(
    subs, slabs, rows, width,
    source, coarse, rho, *refs,
):
    tables, kept = refs[:7], refs[10:17]
    copies = [pltpu.make_async_copy(a, b, refs[17].at[i]) for i, (a, b) in enumerate(zip(tables, kept))]
    run(subs, slabs, rows, width, source, coarse, rho, copies, *kept, *refs[7:10], *refs[18:])


def run(
    subs, slabs, rows, width, source, coarse, rho, copies,
    basis_x, basis_y, basis_z, eigen_x, eigen_y, eigen_z, stiff,
    solved, own_mult, own_jump,
    source_in, coarse_in, sent, lines, spread, got,
    z_right, zt_right, yt_left, xt_left, x_left, x_t, y_t, stiff_t,
    pair_eigen, yz_eigen, x_column, z_column, first_column, last_column,
    y_parts, share_first, share_last, beside, parts_in, half_sum, gathered, gathered_last, ends_in,
    jump_t, search_t, search_in, mult_t, force, edge, sums_out, sums_in,
    in_sem, own_sem, fwd_send, fwd_recv, inv_send, inv_recv, last_send, last_recv,
    part_send, part_recv, mirror_send, mirror_recv, all_send, all_recv, side_send, side_recv, sum_send, sum_recv,
):
    me = lax.axis_index("slab")
    sub = lax.axis_index("sub")
    chunks = rows // TILE
    lanes = min(width, LANES)
    halves = width // lanes
    step_rows = TILE * halves
    ahead = lambda m: lax.rem(me + m, slabs)
    behind = lambda m: lax.rem(me + slabs - m, slabs)
    half = slabs // 2
    block = lax.rem(me, half)
    side = me - block
    mirror = lax.rem(me + half, slabs)
    peer = lambda m: lax.rem(block + m, half)
    next_sub = lax.rem(sub + 1, subs)
    last_sub = lax.rem(sub + subs - 1, subs)
    own_rho = rho[sub]
    weight = 0.5 * (own_rho + rho[next_sub])

    def remote(src, dst, send, recv, target):
        return pltpu.make_async_remote_copy(
            src_ref=src, dst_ref=dst, send_sem=send, recv_sem=recv, device_id=target, device_id_type=MESH
        )

    def fetch(which, g, slot):
        at = pl.ds(g * GROUP, GROUP)
        return (
            pltpu.make_async_copy(source.at[0, at], source_in.at[slot], in_sem.at[0, slot]),
            pltpu.make_async_copy(coarse.at[which, 0, at], coarse_in.at[slot], in_sem.at[1, slot]),
        )

    def start(copies):
        for copy in copies:
            copy.start()

    start(fetch(1, 0, 0))
    start([copies[2], copies[1]])

    barrier = pltpu.get_barrier_semaphore()
    for m in range(1, slabs):
        pl.semaphore_signal(barrier, inc=1, device_id=(sub, ahead(m)), device_id_type=MESH)
    for m in range(1, subs):
        pl.semaphore_signal(barrier, inc=1, device_id=(lax.rem(sub + m, subs), me), device_id_type=MESH)

    start(copies[at] for at in (0, 3, 4, 5, 6))
    copies[2].wait()
    z_right[...] = as_right(basis_z[...])
    copies[1].wait()
    y_t[...] = basis_y[...].T
    yt_left[...] = as_left(y_t[...])

    def forward(m, c, first, count):
        at = pl.ds(first * step_rows, count * step_rows)
        d = ahead(m)
        return remote(
            sent.at[d * chunks + c, at], lines.at[c * slabs + me, at],
            fwd_send.at[c, m], fwd_recv.at[c, m], (sub, d),
        )

    def forward_all(c, first, count):
        for m in range(1, slabs):
            forward(m, c, first, count).start()

    def transform(which, store):
        steps = rows // GROUP

        def step(g, carry):
            slot = lax.rem(g, 2)

            @pl.when(g + 1 < steps)
            def _():
                start(fetch(which, g + 1, 1 - slot))

            for copy in fetch(which, g, slot):
                copy.wait()
            for r in range(GROUP):
                load = source_in[slot, r] + coarse_in[slot, r]
                part = dot(as_left(load), z_right[...])
                part = dot(yt_left[...], as_right(part))
                for h in range(halves):
                    at = pl.ds(pl.multiple_of((g * GROUP + r) * step_rows + h * TILE, TILE), TILE)
                    store[:, at, :] = part[:, h * lanes : (h + 1) * lanes].reshape(width // TILE, TILE, lanes)
            return carry

        return steps, step

    steps, step = transform(1, sent)
    step(0, 0)
    pl.semaphore_wait(barrier, slabs + subs - 2)
    forward_all(0, 0, GROUP)

    def step_and_send(g, carry):
        step(g, carry)
        forward_all(0, g * GROUP, GROUP)
        return carry

    lax.fori_loop(1, steps, step_and_send, 0)
    if chunks > 1:
        forward_all(1, 0, rows)

    keep = lambda c: pltpu.make_async_copy(sent.at[me * chunks + c], lines.at[c * slabs + me], own_sem.at[c])
    for c in range(chunks):
        keep(c).start()

    start(fetch(0, 0, 0))
    for at in (0, 3, 4, 5, 6):
        copies[at].wait()
    square = lambda row: jnp.broadcast_to(row, (width, width))
    down = lambda row: square(row).T
    y_column = down(eigen_y[...])
    pair_eigen[...] = y_column + eigen_x[...]
    yz_eigen[...] = y_column + eigen_z[...]
    x_column[...] = down(eigen_x[...])
    z_column[...] = down(eigen_z[...])
    first_column[...] = down(basis_z[0:1, :])
    last_column[...] = down(basis_z[width - 1 : width, :])
    x_t[...] = basis_x[...].T
    xt_left[...] = as_left(x_t[...])
    x_left[...] = as_left(basis_x[...])
    zt_right[...] = as_right(basis_z[...].T)
    stiff_t[...] = stiff[...].T
    for c in range(chunks):
        own_y = jnp.concatenate([y_t[d * rows + c * TILE : d * rows + (c + 1) * TILE, :] for d in range(slabs)], axis=0)
        y_parts[c] = padded(own_y, True).T.astype(BF16)

    lax.fori_loop(0, *transform(0, spread), 0)
    rest = [(c, q * rows // 4, rows // 4) for c in range(2, chunks) for q in range(4)]
    for piece in rest[:1]:
        forward_all(*piece)

    def line_of(ref, q, at):
        return jnp.concatenate(
            [ref[q, pl.ds(h * TILE + at, rows, stride=step_rows), :] for h in range(halves)], axis=1
        )

    own_x = as_right(basis_x[pl.ds(pl.multiple_of(me * rows, TILE), rows), :])

    def partial_edges(jg, carry):
        at_j = pl.ds(pl.multiple_of(jg * TILE, TILE), TILE)
        eigen = pair_eigen[at_j, :]
        firsts, lasts = [], []
        for at in range(TILE):
            left = as_right_first(line_of(spread, jg, at))
            hat = lax.dot_general(left, own_x, (((0,), (0,)), ((), ())), preferred_element_type=F32)
            modes = hat / (eigen[at : at + 1, :] + z_column[...])
            firsts.append(jnp.sum(modes * first_column[...], axis=0, keepdims=True))
            lasts.append(jnp.sum(modes * last_column[...], axis=0, keepdims=True))
        share_first[at_j, :] = jnp.concatenate(firsts, axis=0) / own_rho
        share_last[at_j, :] = jnp.concatenate(lasts, axis=0) / own_rho
        return carry

    lax.fori_loop(0, width // TILE, partial_edges, 0)

    aside = remote(share_first, beside, side_send.at[0], side_recv.at[0], (last_sub, me))
    aside.start()
    aside.wait()
    share_last[...] = share_last[...] - beside[...]

    own_at = pl.ds(pl.multiple_of(me * rows, TILE), rows)
    lot = width // half
    lot_at = lambda b: pl.ds(pl.multiple_of(b * lot, TILE), lot)
    scatter = [
        remote(share_last.at[lot_at(peer(m))], parts_in.at[m], part_send.at[m], part_recv.at[m], (sub, side + peer(m)))
        for m in range(1, half)
    ]
    start(scatter)
    for piece in rest[1:2]:
        forward_all(*piece)
    total = share_last[lot_at(block), :]
    for m in range(1, half):
        scatter[m - 1].wait_recv()
        total = total + parts_in[m]
    half_sum[...] = total
    swap = remote(half_sum, parts_in.at[0], mirror_send.at[0], mirror_recv.at[0], (sub, mirror))
    swap.start()
    for piece in rest[2:3]:
        forward_all(*piece)
    swap.wait_recv()
    gathered[lot_at(block), :] = total + parts_in[0]
    gather_first = [
        remote(
            gathered.at[lot_at(block)], gathered.at[lot_at(block)], all_send.at[0, m], all_recv.at[0, m],
            (sub, side + peer(m)),
        )
        for m in range(1, half)
    ]
    start(gather_first)
    for piece in rest[3:]:
        forward_all(*piece)
    for copy in gather_first:
        copy.wait_recv()

    def face(it, apart):
        jump = exact(exact(basis_y[...], apart), x_t[...])
        modes = exact(exact(y_t[...], jump), basis_x[...]) * stiff_t[...]
        search = exact(exact(basis_y[...], modes), x_t[...]) * weight
        jump_t[...] = jump
        search_t[it] = search
        both = jnp.sum(jump * search, axis=(0, 1), keepdims=True)
        norm = jnp.sum(search * search, axis=(0, 1), keepdims=True)
        line = lax.broadcasted_iota(jnp.int32, (TILE, LANES), 0)
        sums_out[it] = jnp.where(line == 0, both, norm)

    def sums(it):
        return [
            remote(
                sums_out.at[it], sums_in.at[it, m], sum_send.at[it, m], sum_recv.at[it, m],
                (lax.rem(sub + m, subs), me),
            )
            for m in range(1, subs)
        ]

    def step_length(it, copies):
        total = sums_out[it]
        for m in range(1, subs):
            copies[m - 1].wait_recv()
            total = total + sums_in[it, m]
        return total[0:1, 0:1] / (total[1:2, 0:1] + 1e-06)

    face(0, gathered[...])
    sums_first = sums(0)
    start(sums_first)
    pass_on = remote(search_t.at[0], search_in, side_send.at[1], side_recv.at[1], (next_sub, me))
    pass_on.start()
    alpha = step_length(0, sums_first)
    mult_t[...] = alpha * search_t[0]
    force[1] = exact(exact(y_t[...], -mult_t[...]), basis_x[...]).T
    pass_on.wait_recv()
    force[0] = exact(exact(y_t[...], alpha * search_in[...]), basis_x[...]).T

    edge[...] = jnp.zeros_like(edge)

    def modal(c):
        def one(at, carry):
            mine = c * TILE + at
            j = me * rows + mine
            line = jnp.concatenate([line_of(lines, c * slabs + d, at) for d in range(slabs)], axis=0)
            hat = dot(xt_left[...], as_right(line))
            lane = lax.broadcasted_iota(jnp.int32, (width, width), 1)
            pick = lambda p: jnp.sum(jnp.where(lane == j, force[p], 0.0), axis=1, keepdims=True)
            hat = hat + pick(0) * basis_z[0:1, :] + pick(1) * basis_z[width - 1 : width, :]
            modes = hat / ((x_column[...] + yz_eigen[pl.ds(j, 1), :]) * own_rho)
            back = dot(x_left[...], as_right(modes))
            for d in range(slabs):
                for h in range(halves):
                    at_x = pl.ds(h * TILE + at, rows, stride=step_rows)
                    spread[c * slabs + d, at_x, :] = back[d * rows : (d + 1) * rows, h * lanes : (h + 1) * lanes]
            lane = lax.broadcasted_iota(jnp.int32, (width, LANES), 1)
            first = jnp.sum(modes * basis_z[0:1, :], axis=1, keepdims=True)
            last = jnp.sum(modes * basis_z[width - 1 : width, :], axis=1, keepdims=True)
            edge[...] += jnp.where(lane == mine, first, 0.0) + jnp.where(lane == rows + mine, last, 0.0)
            return carry

        for m in range(1, slabs):
            d = behind(m)
            remote(
                sent.at[d * chunks + c], lines.at[c * slabs + d], fwd_send.at[c, m], fwd_recv.at[c, m], (sub, d)
            ).wait_recv()
        keep(c).wait()
        lax.fori_loop(0, TILE, one, 0)

    last = chunks - 1
    pieces = PIECES
    quarter = rows // pieces
    quarters = [pl.ds(q * quarter * step_rows, quarter * step_rows) for q in range(pieces)]

    def inverse(c, m, q=None):
        d = ahead(m)
        src, dst = spread.at[c * slabs + d], got.at[c * slabs + me]
        if q is None:
            return remote(src, dst, inv_send.at[c, m], inv_recv.at[c, m], (sub, d))
        return remote(src.at[quarters[q]], dst.at[quarters[q]], last_send.at[q, m], last_recv.at[q, m], (sub, d))

    def inverse_from(c, m, q=None):
        d = behind(m)
        src, dst = spread.at[c * slabs + d], got.at[c * slabs + d]
        if q is None:
            return remote(src, dst, inv_send.at[c, m], inv_recv.at[c, m], (sub, d))
        return remote(src.at[quarters[q]], dst.at[quarters[q]], last_send.at[q, m], last_recv.at[q, m], (sub, d))

    stay = lambda c: pltpu.make_async_copy(spread.at[c * slabs + me], got.at[c * slabs + me], own_sem.at[c])
    back = []

    def give(c):
        copies = [inverse(c, m, q) for q in (range(pieces) if c == last else [None]) for m in range(slabs - 1, 0, -1)]
        start(copies)
        back.extend(copies)

    for c in range(chunks):
        modal(c)
        stay(c).start()
        if c == 0 and last > 0:
            give(c)

    edge_t = edge[...].T
    ends_in[0] = edge_t[:rows]
    send_ends = remote(ends_in.at[0], ends_in.at[1], side_send.at[2], side_recv.at[2], (last_sub, me))
    send_ends.start()
    send_ends.wait_recv()
    gathered_last[own_at, :] = edge_t[rows : 2 * rows] - ends_in[1]
    far_at = pl.ds(pl.multiple_of(mirror * rows, TILE), rows)

    def hand(at, k, m, target):
        return remote(gathered_last.at[at], gathered_last.at[at], all_send.at[k, m], all_recv.at[k, m], (sub, target))

    swap_last = remote(
        gathered_last.at[own_at], gathered_last.at[own_at], mirror_send.at[1], mirror_recv.at[1], (sub, mirror)
    )
    swap_last.start()
    gather_own = [hand(own_at, 1, m, side + peer(m)) for m in range(1, half)]
    gather_far = [hand(far_at, 2, m, side + peer(m)) for m in range(1, half)]
    start(gather_own)
    for c in range(1, min(2, last)):
        give(c)

    def finish(c, q):
        at = pl.ds(pl.multiple_of(q * quarter * step_rows, TILE), quarter * step_rows)
        whole = got[pl.ds(c * slabs, slabs), at, :].reshape(slabs * quarter, halves, TILE, lanes)
        whole = [whole[:, h].reshape(slabs * quarter * TILE, lanes) for h in range(halves)]
        whole = dot(as_left(jnp.concatenate(whole, axis=1)), zt_right[...])
        whole = whole.reshape(slabs, quarter, TILE, width)
        for r in range(quarter):
            part = dot(y_parts[c], padded(whole[:, r].reshape(slabs * TILE, width), False).astype(BF16))
            x = q * quarter + r
            solved[x] = part if c == 0 else solved[x] + part

    def arrive(c):
        stay(c).wait()
        if c < last:
            for m in range(1, slabs):
                inverse_from(c, m).wait_recv()

            def one(q, carry):
                finish(c, q)
                return carry

            lax.fori_loop(0, pieces, one, 0)
        else:
            for q in range(pieces):
                for m in range(1, slabs):
                    inverse_from(c, m, q).wait_recv()
                finish(c, q)

    if last > 0:
        arrive(0)
    swap_last.wait_recv()
    start(gather_far)
    for c in range(min(2, last), chunks):
        give(c)
    for c in range(1, last - 1):
        arrive(c)
    for copy in gather_own + gather_far:
        copy.wait_recv()
    face(1, gathered_last[...])
    sums_last = sums(1)
    start(sums_last)
    alpha = step_length(1, sums_last)
    mult_t[...] = (mult_t[...] + alpha * search_t[1]).T
    own_mult[...] = mult_t[own_at, :]
    jump_t[...] = jump_t[...].T
    own_jump[...] = jump_t[own_at, :]

    small = [scatter, [swap, swap_last, pass_on, send_ends], gather_first, gather_own, gather_far, sums_first, sums_last]
    for copies in small:
        for copy in copies:
            copy.wait_send()
    for c in range(chunks):
        for m in range(1, slabs):
            forward(m, c, 0, rows).wait_send()

    for c in range(max(1, last - 1) if last else 0, chunks):
        arrive(c)
    for copy in back:
        copy.wait_send()


def padded(value, left):
    top = value.astype(BF16).astype(F32)
    low = value - top
    parts = [top, top, low] if left else [top, low, top]
    over = -3 * value.shape[0] % LANES
    if over:
        parts.append(jnp.zeros((over, value.shape[1]), F32))
    return jnp.concatenate(parts, axis=0)


def as_right_first(value):
    top, low = split(value)
    return jnp.concatenate([top, top, low], axis=0)


def iterate(subs, slabs, source, coarse, rho, basis_x, basis_y, basis_z, eigen_x, eigen_y, eigen_z, stiff):
    rows, width = source.shape[1:3]
    chunks = rows // TILE
    face = lambda *lead: pltpu.VMEM((*lead, width, width), F32)
    lot = lambda *lead: pltpu.VMEM((*lead, rows, width), F32)
    lanes = min(width, LANES)
    field = lambda: pltpu.VMEM((chunks * slabs, TILE * rows * (width // lanes), lanes), F32)
    half = slabs // 2
    stack = 3 * slabs * TILE
    stack += -stack % LANES
    line = pltpu.VMEM((1, width), F32)
    dma = pltpu.SemaphoreType.DMA
    vmem = pl.BlockSpec(memory_space=pltpu.VMEM)
    hbm = pl.BlockSpec(memory_space=pl.ANY)
    return pl.pallas_call(
        functools.partial(feti_kernel, subs, slabs, rows, width),
        out_shape=(
            pltpu.VMEM((rows, width, width), F32),
            pltpu.VMEM((rows, width), F32),
            pltpu.VMEM((rows, width), F32),
        ),
        in_specs=[hbm, hbm, pl.BlockSpec(memory_space=pltpu.SMEM)] + [hbm] * 7,
        out_specs=(vmem, vmem, vmem),
        scratch_shapes=[
            face(), face(), face(), line, line, line, face(), dma((7,)),
            face(2, GROUP), face(2, GROUP), field(), field(), field(), field(),
            pltpu.VMEM((3 * width, width), BF16), pltpu.VMEM((3 * width, width), BF16),
            pltpu.VMEM((width, 3 * width), BF16), pltpu.VMEM((width, 3 * width), BF16),
            pltpu.VMEM((width, 3 * width), BF16), face(), face(), face(),
            face(), face(), face(), face(), face(), face(),
            pltpu.VMEM((chunks, width, stack), BF16),
            face(), face(), face(), pltpu.VMEM((half, width // half, width), F32),
            pltpu.VMEM((width // half, width), F32), face(), face(), lot(2),
            face(), face(ITERS), face(), face(), face(2), pltpu.VMEM((width, LANES), F32),
            pltpu.VMEM((ITERS, TILE, LANES), F32), pltpu.VMEM((ITERS, subs, TILE, LANES), F32),
            dma((2, 2)), dma((chunks,)),
            dma((chunks, slabs)), dma((chunks, slabs)), dma((chunks, slabs)), dma((chunks, slabs)),
            dma((PIECES, slabs)), dma((PIECES, slabs)),
            dma((half,)), dma((half,)), dma((2,)), dma((2,)), dma((3, half)), dma((3, half)),
            dma((3,)), dma((3,)), dma((ITERS, subs)), dma((ITERS, subs)),
        ],
        compiler_params=pltpu.CompilerParams(
            collective_id=0, has_side_effects=True, vmem_limit_bytes=54 * 2**20
        ),
        name="feti",
    )(source, coarse, rho, basis_x, basis_y, basis_z, eigen_x, eigen_y, eigen_z, stiff)


def hand_out_kernel(*refs):
    count = len(refs) // 2
    copies = []
    for i in range(count):
        parts = min(HAND_OUT, refs[i].shape[0]) if i == 0 else 1
        lot = refs[i].shape[0] // parts
        for part in range(parts):
            at = pl.ds(part * lot, lot)
            copies.append(pltpu.make_async_copy(refs[i].at[at], refs[count + i].at[at], refs[-1].at[len(copies)]))
    for copy in copies:
        copy.start()
    for copy in copies:
        copy.wait()


def hand_out(*results):
    anywhere = pl.BlockSpec(memory_space=pl.ANY)
    return pl.pallas_call(
        hand_out_kernel,
        out_shape=[pltpu.HBM(value.shape, value.dtype) for value in results],
        in_specs=[anywhere] * len(results),
        out_specs=[anywhere] * len(results),
        scratch_shapes=[pltpu.SemaphoreType.DMA((HAND_OUT + len(results),))],
        compiler_params=pltpu.CompilerParams(vmem_limit_bytes=2**20),
        name="hand_out",
    )(*(pltpu.with_memory_space_constraint(value, pltpu.VMEM) for value in results))


def on_device(
    source, coarse, rho, basis_x, basis_y, basis_z, eigen_x, eigen_y, eigen_z, face_stiff
):
    subs = lax.axis_size("sub")
    slabs = lax.axis_size("slab")
    solved, multipliers, jump = iterate(
        subs, slabs, source, coarse, rho, basis_x, basis_y, basis_z,
        eigen_x[None], eigen_y[None], eigen_z[None], face_stiff,
    )
    solved, multipliers, jump = hand_out(solved, multipliers, jump)
    return (solved[None], multipliers[None], jump[None])


def solution(mesh):
    in_specs = (
        P("sub", "slab", None, None),
        P(None, "sub", "slab", None, None),
        P(),
        P(),
        P(),
        P(),
        P(),
        P(),
        P(),
        P(),
    )
    out_specs = (P("sub", "slab", None, None), P("sub", "slab", None), P("sub", "slab", None))
    return jax.shard_map(
        on_device, mesh=mesh, in_specs=in_specs, out_specs=out_specs, check_vma=False
    )
```
